128 devices in a mesh: freq: 16 (over y, x_hi, core), row: 4 (over z), col: 2 (over x_lo).
Axes of the slice: x: 4 (x_hi: 2, x_lo: 2; x = x_hi * 2 + x_lo), y: 4, z: 4, core: 2. Of those that a mesh axis runs over, the one named last changes fastest.
Arguments:
- voltages: bfloat16 [512, 259, 2048], P(('row', 'col', 'freq')), may hold values from -128 to 127, as said below
- tap_table: int32 [4, 2048], replicated, may hold values from -4096 to 4095
Outputs:
- visibility: float32 [1024, 2, 4, 128, 512], P('freq', None, None, 'col', 'row')
The draws below stay inside these ranges and needn't reach their ends.
Inputs may be any that keep to these rules, and one draw needn't show every extreme that they name: `voltages`: whole numbers.
All inputs are finite; a program needn't handle non-finite values.
Results may differ from the reference program's by a relative error of at most 0.0033.
Values may be sent and summed in bfloat16 or wider, within the bound.
A program may use at most 192 MiB of HBM per device.

```python
import math
import jax
import jax.numpy as jnp
from jax import lax

NFFT = 2048
TAPS = 4
SPEC = 256
CHAN = 1024
INPUTS = 512
FRAMES = 259
N_ROW = 4


def draw_voltages(key, part):
    shape = (INPUTS, FRAMES, NFFT)
    values = jax.random.randint(jax.random.fold_in(key, 10), shape, -128, 128)
    return values.astype(jnp.float32).astype(jnp.bfloat16)


def plant(drawn, rng, low, top_value):
    longest = drawn.shape.index(max(drawn.shape))
    spots = []
    for shift in (0, 1):
        where = [jax.random.randint(jax.random.fold_in(rng, axis), (), 0, length) for axis, length in enumerate(drawn.shape)]
        where[longest] = (where[longest] + shift) % drawn.shape[longest]
        spots.append(tuple(where))
    return drawn.at[spots[0]].set(low).at[spots[1]].set(top_value)


def setup_inputs(seed: int = 0) -> dict:
    key_of = jax.random.split(jax.random.key(seed), 3)
    voltages = draw_voltages(jax.random.fold_in(key_of[2], 71), 0)
    tap_table = plant(jax.random.randint(key_of[1], (TAPS, NFFT), -4096, 4096), jax.random.fold_in(key_of[1], 1), -4096, 4095).astype(jnp.int32)
    return dict(voltages=voltages, tap_table=tap_table)


def filter_block(volt_rows, tap_table):
    weights = tap_table.astype(jnp.float32) / 4096.0
    filtered = weights[0] * volt_rows[:, 0:SPEC, :].astype(jnp.float32)
    for tap_index in range(1, TAPS):
        filtered = filtered + weights[tap_index] * volt_rows[:, tap_index:tap_index + SPEC, :].astype(jnp.float32)
    spectrum = jnp.fft.rfft(filtered, axis=-1)[..., :CHAN] / (64.0 * math.sqrt(NFFT))
    return (jnp.real(spectrum).astype(jnp.bfloat16), jnp.imag(spectrum).astype(jnp.bfloat16))

def correlate_block(pair):
    real_rows = pair[0].astype(jnp.float32)
    imag_rows = pair[1].astype(jnp.float32)
    highest = lax.Precision.HIGHEST
    real_vis = jnp.einsum('cjt,cit->cji', real_rows, real_rows, precision=highest) + jnp.einsum('cjt,cit->cji', imag_rows, imag_rows, precision=highest)
    imag_vis = jnp.einsum('cjt,cit->cji', real_rows, imag_rows, precision=highest) - jnp.einsum('cjt,cit->cji', imag_rows, real_rows, precision=highest)
    return jnp.stack([real_vis, imag_vis], axis=1) / SPEC

def reference(voltages, tap_table):
    blocks = voltages.reshape(INPUTS // 16, 16, FRAMES, NFFT)
    real_part, imag_part = lax.map(lambda volt_rows: filter_block(volt_rows, tap_table), blocks)
    real_part = real_part.reshape(INPUTS, SPEC, CHAN).transpose(2, 0, 1).reshape(CHAN // 8, 8, INPUTS, SPEC)
    imag_part = imag_part.reshape(INPUTS, SPEC, CHAN).transpose(2, 0, 1).reshape(CHAN // 8, 8, INPUTS, SPEC)
    result = lax.map(correlate_block, (real_part, imag_part))
    return result.reshape(CHAN, 2, N_ROW, INPUTS // N_ROW, INPUTS)
```

```python
import functools
import math

import jax
import jax.numpy as jnp
import ml_dtypes
import numpy as np
from jax import lax
from jax.experimental import pallas as pl
from jax.experimental.pallas import tpu as pltpu
from jax.sharding import PartitionSpec as P

NFFT = 2048
HALF = NFFT // 2
TAPS = 4
SPEC = 256
CHAN = 1024
GROUPS = 16
LOCAL_CHAN = CHAN // GROUPS
CHUNKS = 4
CHUNK_CHAN = LOCAL_CHAN // CHUNKS
FOLD_CHAN = CHUNK_CHAN // 2
TARGETS = 8
ROWS = 2 * TARGETS * FOLD_CHAN
F32 = jnp.float32
BF16 = jnp.bfloat16
MESH = pl.DeviceIdType.MESH


def dft_tables():
    core, chunk, parity, part, target, index = np.meshgrid(
        np.arange(2), np.arange(CHUNKS), np.arange(2), np.arange(2), np.arange(TARGETS), np.arange(FOLD_CHAN),
        indexing="ij",
    )
    channel = (target * 2 + core) * LOCAL_CHAN + chunk * CHUNK_CHAN + 2 * index + parity
    phase = (channel[..., None] * np.arange(HALF)) % NFFT
    angle = phase * (2.0 * np.pi / NFFT)
    cosine = np.where(phase % (NFFT // 2) == NFFT // 4, 0.0, np.cos(angle))
    sine = np.where(phase % (NFFT // 2) == 0, 0.0, np.sin(angle))
    values = np.where(part[..., None] == 0, cosine, -sine) / (64.0 * math.sqrt(NFFT) * 4096.0)
    high = values.astype(ml_dtypes.bfloat16)
    low = (values - high.astype(np.float64)).astype(ml_dtypes.bfloat16)
    shape = (2, CHUNKS, 2, ROWS, HALF)
    return np.concatenate([high.reshape(shape), low.reshape(shape)], axis=3)


def spectrum_kernel(core_ref, own_ref, other_ref, weight_ref, table_ref, out_ref, frames, folded, turned):
    core = core_ref[0]

    @pl.when(pl.program_id(0) == 0)
    def _():
        for source, first in ((own_ref, 0), (other_ref, 4)):

            @pl.loop(0, 4 * (HALF // 128))
            def _(step):
                row = step // (HALF // 128)
                low = pl.multiple_of((step % (HALF // 128)) * 128, 128)
                high = pl.multiple_of(low + HALF, 128)
                count = SPEC + TAPS - 1
                frames[0, 0:count, :] = source[row, :, pl.ds(low, 128)].astype(F32)
                frames[1, 0:count, :] = source[row, :, pl.ds(high, 128)].astype(F32)
                for start in range(0, SPEC, 64):
                    halves = []
                    for half, column in ((0, low), (1, high)):
                        total = None
                        for tap in range(TAPS):
                            weight = weight_ref[pl.ds(tap, 1), pl.ds(column, 128)]
                            term = weight * frames[half, start + tap : start + tap + 64, :]
                            total = term if total is None else total + term
                        halves.append(total)
                    for parity, value in ((0, halves[0] + halves[1]), (1, halves[0] - halves[1])):
                        top = value.astype(BF16)
                        rest = (value - top.astype(F32)).astype(BF16)
                        folded[parity, 0, first + row, start : start + 64, pl.ds(low, 128)] = top
                        folded[parity, 1, first + row, start : start + 64, pl.ds(low, 128)] = rest

    contract = (((1,), (1,)), ((), ()))

    @pl.loop(0, 8)
    def _(slot):
        row = lax.rem(slot + 4 * core, 8)
        for parity in range(2):
            top = folded[parity, 0, slot]
            both = lax.dot_general(table_ref[0, 0, parity], top, contract, preferred_element_type=F32)
            rest = lax.dot_general(
                table_ref[0, 0, parity, :ROWS], folded[parity, 1, slot], contract, preferred_element_type=F32
            )
            value = both[:ROWS] + both[ROWS:] + rest
            for part in range(2):
                for target in range(TARGETS):
                    first = (part * TARGETS + target) * FOLD_CHAN
                    start = target * (CHUNK_CHAN * 16) + parity * 16 + part * 8 + row
                    for half in range(2):
                        turned[half, pl.ds(start, FOLD_CHAN, stride=32), :] = value[
                            first : first + FOLD_CHAN, half * 128 : half * 128 + 128
                        ]

    block = CHUNK_CHAN * 16

    @pl.loop(0, TARGETS)
    def _(target):
        for half in range(2):
            rows = turned[half, pl.ds(pl.multiple_of(target * block, block), block), :]
            out_ref[0, target, :, :, half * 128 : half * 128 + 128] = rows.reshape(2 * CHUNK_CHAN, 8, 128).astype(BF16)


def spectra(own, other, weights, table, core):
    whole = lambda shape: pl.BlockSpec(shape, lambda k, c: (0,) * len(shape))
    return pl.pallas_call(
        spectrum_kernel,
        grid_spec=pltpu.PrefetchScalarGridSpec(
            num_scalar_prefetch=1,
            grid=(CHUNKS,),
            in_specs=[
                whole(own.shape),
                whole(other.shape),
                whole(weights.shape),
                pl.BlockSpec((1, 1, 2, 2 * ROWS, HALF), lambda k, c: (c[0], k, 0, 0, 0)),
            ],
            out_specs=pl.BlockSpec((1, TARGETS, 2 * CHUNK_CHAN, 8, SPEC), lambda k, c: (k, 0, 0, 0, 0)),
            scratch_shapes=[
                pltpu.VMEM((2, 272, 128), F32),
                pltpu.VMEM((2, 2, 8, SPEC, HALF), BF16),
                pltpu.VMEM((2, TARGETS * CHUNK_CHAN * 16, 128), F32),
            ],
        ),
        out_shape=jax.ShapeDtypeStruct((CHUNKS, TARGETS, 2 * CHUNK_CHAN, 8, SPEC), BF16),
        compiler_params=pltpu.CompilerParams(vmem_limit_bytes=56 << 20),
        name="spectra",
    )(core, own, other, weights, table)


def exchange_kernel(
    spec_ref, rows, planes, local_sem, first_send, first_recv, pair_send, pair_recv, ring_send, ring_recv, pass_send, pass_recv
):
    freq, z, xl = lax.axis_index("freq"), lax.axis_index("row"), lax.axis_index("col")
    core = lax.rem(freq, 2)
    xh = lax.rem(freq // 2, 2)
    y = freq // 4
    up, down = lax.rem(z + 1, 4), lax.rem(z + 3, 4)

    def device(to_y, to_xh, to_z, to_xl):
        return {"freq": (to_y * 2 + to_xh) * 2 + core, "row": to_z, "col": to_xl}

    partner = device(y, xh, z, 1 - xl)
    above, below = device(y, xh, up, xl), device(y, xh, down, xl)

    barrier = pltpu.get_barrier_semaphore()
    others = [device(lax.rem(y + step, 4), xh, z, xl) for step in range(1, 4)]
    others += [device(lax.rem(y + step, 4), 1 - xh, z, 1 - xl) for step in range(4)]
    others += [partner, above, below]
    for other in others:
        pl.semaphore_signal(barrier, inc=1, device_id=other, device_id_type=MESH)
    pl.semaphore_wait(barrier, len(others))

    def remote(source, target, send, recv, where):
        return pltpu.make_async_remote_copy(
            src_ref=source, dst_ref=target, send_sem=send, recv_sem=recv, device_id=where, device_id_type=MESH
        )

    def first(k, step, flip):
        to_y, to_xh, to_xl = lax.rem(y + step, 4), (1 - xh if flip else xh), (1 - xl if flip else xl)
        index = flip * 4 + step
        return remote(
            spec_ref.at[k, to_y * 2 + to_xh],
            rows.at[k, :, xl, y, xh],
            first_send.at[k, index],
            first_recv.at[k, index],
            device(to_y, to_xh, z, to_xl),
        )

    def first_arrival(k, step, flip):
        from_y, from_xh, from_xl = lax.rem(y + 4 - step, 4), (1 - xh if flip else xh), (1 - xl if flip else xl)
        index = flip * 4 + step
        place = rows.at[k, :, from_xl, from_y, from_xh]
        return remote(place, place, first_send.at[k, index], first_recv.at[k, index], device(from_y, from_xh, z, from_xl))

    def local(k):
        return pltpu.make_async_copy(spec_ref.at[k, y * 2 + xh], rows.at[k, :, xl, y, xh], local_sem.at[k])

    def block(k, part, mine):
        side = xl if part == 0 else 1 - xl
        if not mine:
            side = 1 - side
        return rows.at[k, :, side, :, xh if part == 0 else 1 - xh]

    def pair(k, part, mine=True):
        place = block(k, part, mine)
        return remote(place, place, pair_send.at[k, part], pair_recv.at[k, part], partner)

    def ring(k, part, way):
        column = xh if part == 0 else 1 - xh
        return remote(
            rows.at[k, :, xl, :, column],
            planes.at[way, k, :, :, column],
            ring_send.at[k, part, way],
            ring_recv.at[k, part, way],
            above if way == 0 else below,
        )

    def onward(k, part):
        column = xh if part == 0 else 1 - xh
        return remote(
            planes.at[part, k, :, :, column],
            planes.at[2, k, :, :, column],
            pass_send.at[k, part],
            pass_recv.at[k, part],
            above if part == 0 else below,
        )

    for k in range(CHUNKS):
        local(k).start()
        for step in range(1, 4):
            first(k, step, 0).start()
        for step in range(4):
            first(k, step, 1).start()

    for turn in range(CHUNKS + 2):
        k = turn
        if k < CHUNKS:
            local(k).wait()
            for step in range(1, 4):
                first_arrival(k, step, 0).wait_recv()
            for way in range(2):
                ring(k, 0, way).start()
            pair(k, 0).start()
            for step in range(4):
                first_arrival(k, step, 1).wait_recv()
            pair(k, 1).start()
        k = turn - 1
        if 0 <= k < CHUNKS:
            pair(k, 1, False).wait_recv()
            for way in range(2):
                ring(k, 1, way).start()
        k = turn - 2
        if 0 <= k < CHUNKS:
            for part in range(2):
                ring(k, part, part).wait_recv()
                onward(k, part).start()

    for k in range(CHUNKS):
        pair(k, 0, False).wait_recv()
        for part in range(2):
            ring(k, part, 1 - part).wait_recv()
            onward(k, part).wait_recv()
    for k in range(CHUNKS):
        for step in range(1, 4):
            first(k, step, 0).wait_send()
        for step in range(4):
            first(k, step, 1).wait_send()
        for part in range(2):
            pair(k, part).wait_send()
            for way in range(2):
                ring(k, part, way).wait_send()
            onward(k, part).wait_send()


def exchange(spec):
    any_space = pl.BlockSpec(memory_space=pl.ANY)
    dma = pltpu.SemaphoreType.DMA
    return pl.pallas_call(
        exchange_kernel,
        in_specs=[any_space],
        out_specs=[any_space, any_space],
        out_shape=[
            jax.ShapeDtypeStruct((CHUNKS, 2 * CHUNK_CHAN, 2, 4, 2, 8, SPEC), BF16),
            jax.ShapeDtypeStruct((3, CHUNKS, 2 * CHUNK_CHAN, 4, 2, 8, SPEC), BF16),
        ],
        scratch_shapes=[
            dma((CHUNKS,)),
            dma((CHUNKS, 8)),
            dma((CHUNKS, 8)),
            dma((CHUNKS, 2)),
            dma((CHUNKS, 2)),
            dma((CHUNKS, 2, 2)),
            dma((CHUNKS, 2, 2)),
            dma((CHUNKS, 2)),
            dma((CHUNKS, 2)),
        ],
        compiler_params=pltpu.CompilerParams(collective_id=0, has_side_effects=True),
        name="exchange",
    )(spec)


def correlate_kernel(step_chan, place_ref, rows_ref, planes_ref, out_ref):
    z, xl = place_ref[0], place_ref[1]
    for c in range(step_chan):
        real, imag = rows_ref[c, 0], rows_ref[c, 1]
        weights = jnp.concatenate(
            [jnp.concatenate([real, imag], axis=1), jnp.concatenate([imag, -real], axis=1)], axis=0
        )
        start = pl.multiple_of(xl * 64, 64)
        pieces = [jnp.concatenate([rows_ref[c, 0, pl.ds(start, 64)], rows_ref[c, 1, pl.ds(start, 64)]], axis=1)]
        for slot in range(3):
            pieces.append(jnp.concatenate([planes_ref[slot, c, 0], planes_ref[slot, c, 1]], axis=1))
        for piece, shift in zip(pieces, (0, 3, 1, 2)):
            value = lax.dot_general(piece, weights, (((1,), (1,)), ((), ())), preferred_element_type=F32) * (1.0 / SPEC)
            plane = lax.rem(z + shift, 4)
            out_ref[c, 0, plane] = value[:, :128]
            out_ref[c, 1, plane] = value[:, 128:]


def correlate(rows, planes, place):
    step_chan = 4
    return pl.pallas_call(
        functools.partial(correlate_kernel, step_chan),
        grid_spec=pltpu.PrefetchScalarGridSpec(
            num_scalar_prefetch=1,
            grid=(LOCAL_CHAN // step_chan,),
            in_specs=[
                pl.BlockSpec((step_chan, 2, 128, SPEC), lambda g, p: (g, 0, 0, 0)),
                pl.BlockSpec((3, step_chan, 2, 64, SPEC), lambda g, p: (0, g, 0, 0, 0)),
            ],
            out_specs=pl.BlockSpec((step_chan, 2, 4, 64, 128), lambda g, p: (g, 0, 0, 0, 0)),
        ),
        out_shape=jax.ShapeDtypeStruct((LOCAL_CHAN, 2, 4, 64, 128), F32),
        compiler_params=pltpu.CompilerParams(vmem_limit_bytes=40 << 20),
        name="correlate",
    )(place, rows, planes)


def shards(table, voltages, tap_table):
    freq, z, xl = lax.axis_index("freq"), lax.axis_index("row"), lax.axis_index("col")
    weights = tap_table.astype(F32)
    other = lax.ppermute(voltages, "freq", [(f, f ^ 1) for f in range(GROUPS)])
    core = (freq % 2).astype(jnp.int32).reshape(1)
    spec = spectra(voltages, other, weights, table, core)
    rows, planes = exchange(spec)
    rows = rows.reshape(LOCAL_CHAN, 2, 128, SPEC)
    planes = planes.reshape(3, LOCAL_CHAN, 2, 64, SPEC)
    return correlate(rows, planes, jnp.stack([z, xl]).astype(jnp.int32))


def solution(mesh):
    table = dft_tables()

    def run(voltages, tap_table):
        return jax.shard_map(
            shards,
            mesh=mesh,
            in_specs=(P(), P(("row", "col", "freq"), None, None), P()),
            out_specs=P("freq", None, None, "col", "row"),
            check_vma=False,
        )(jnp.asarray(table), voltages, tap_table)

    return run
```

```python
import math

import jax
import jax.numpy as jnp
import ml_dtypes
import numpy as np
from jax import lax
from jax.experimental import pallas as pl
from jax.experimental.pallas import tpu as pltpu
from jax.sharding import PartitionSpec as P

NFFT = 2048
HALF = NFFT // 2
TAPS = 4
SPEC = 256
CHAN = 1024
GROUPS = 16
LOCAL_CHAN = CHAN // GROUPS
CHUNKS = 4
CHUNK_CHAN = LOCAL_CHAN // CHUNKS
FOLD_CHAN = CHUNK_CHAN // 2
TARGETS = 8
ROWS = 2 * TARGETS * FOLD_CHAN
HALF_SPEC = SPEC // 2
STEPS = 2 * CHUNKS
STEP_CHAN = 4
F32 = jnp.float32
BF16 = jnp.bfloat16
MESH = pl.DeviceIdType.MESH


def dft_tables():
    core, chunk, parity, part, target, index = np.meshgrid(
        np.arange(2), np.arange(CHUNKS), np.arange(2), np.arange(2), np.arange(TARGETS), np.arange(FOLD_CHAN),
        indexing="ij",
    )
    channel = (target * 2 + core) * LOCAL_CHAN + chunk * CHUNK_CHAN + 2 * index + parity
    phase = (channel[..., None] * np.arange(HALF)) % NFFT
    angle = phase * (2.0 * np.pi / NFFT)
    cosine = np.where(phase % (NFFT // 2) == NFFT // 4, 0.0, np.cos(angle))
    sine = np.where(phase % (NFFT // 2) == 0, 0.0, np.sin(angle))
    values = np.where(part[..., None] == 0, cosine, -sine) / (64.0 * math.sqrt(NFFT) * 4096.0)
    high = values.astype(ml_dtypes.bfloat16)
    low = (values - high.astype(np.float64)).astype(ml_dtypes.bfloat16)
    shape = (2, CHUNKS, 2, ROWS, HALF)
    return np.concatenate([high.reshape(shape), low.reshape(shape)], axis=3)


def filter_half(half, source, first, weight_ref, frames, folded):
    count = HALF_SPEC + TAPS - 1

    @pl.loop(0, HALF // 128)
    def _(step):
        low = pl.multiple_of(step * 128, 128)
        columns = (low, pl.multiple_of(low + HALF, 128))
        for side in range(2):
            block = source[pl.ds(half * HALF_SPEC, count), :, pl.ds(columns[side], 128)]
            frames[side, 0 : 4 * count, :] = block.astype(F32).reshape(4 * count, 128)
        for row in range(4):
            slot = first + row
            for start in range(0, HALF_SPEC, 64):
                sides = []
                for side in range(2):
                    total = None
                    for tap in range(TAPS):
                        weight = weight_ref[pl.ds(tap, 1), pl.ds(columns[side], 128)]
                        term = weight * frames[side, pl.ds((start + tap) * 4 + row, 64, stride=4), :]
                        total = term if total is None else total + term
                    sides.append(total)
                place = (slot % 2) * HALF_SPEC + start
                for parity, value in ((0, sides[0] + sides[1]), (1, sides[0] - sides[1])):
                    top = value.astype(BF16)
                    rest = (value - top.astype(F32)).astype(BF16)
                    folded[parity, 0, half, slot // 2, place : place + 64, pl.ds(low, 128)] = top
                    folded[parity, 1, half, slot // 2, place : place + 64, pl.ds(low, 128)] = rest


def transform_chunk(half, quarter, core, table_ref, folded, turned, write):
    contract = (((1,), (1,)), ((), ()))

    @pl.loop(0, 4)
    def _(duo):
        for parity in range(2):
            top = folded[parity, 0, half, duo]
            both = lax.dot_general(table_ref[quarter, parity], top, contract, preferred_element_type=F32)
            rest = lax.dot_general(
                table_ref[quarter, parity, :ROWS], folded[parity, 1, half, duo], contract, preferred_element_type=F32
            )
            value = both[:ROWS] + both[ROWS:] + rest
            for sub in range(2):
                row = lax.rem(2 * duo + sub + 4 * core, 8)
                for part in range(2):
                    turned[pl.ds(parity * 16 + part * 8 + row, ROWS // 2, stride=32), :] = value[
                        part * (ROWS // 2) : (part + 1) * (ROWS // 2), sub * 128 : sub * 128 + 128
                    ]

    block = CHUNK_CHAN * 16

    @pl.loop(0, TARGETS)
    def _(target):
        rows = turned[pl.ds(pl.multiple_of(target * block, block), block), :]
        write(target, rows.reshape(2 * CHUNK_CHAN, 8, 128).astype(BF16))


def exchange_kernel(
    own_ref, weight_ref, table_hbm, rows, planes,
    own, other, table, frames, folded, turned, made,
    load_sem, table_sem, core_send, core_recv,
    local_sem, first_send, first_recv, pair_send, pair_recv, ring_send, ring_recv, pass_send, pass_recv,
):
    freq, z, xl = lax.axis_index("freq"), lax.axis_index("row"), lax.axis_index("col")
    core = lax.rem(freq, 2)
    xh = lax.rem(freq // 2, 2)
    y = freq // 4
    up, down = lax.rem(z + 1, 4), lax.rem(z + 3, 4)
    pieces = (pl.ds(0, HALF_SPEC + TAPS - 1), pl.ds(HALF_SPEC + TAPS - 1, HALF_SPEC))

    def load(part):
        return pltpu.make_async_copy(own_ref.at[pieces[part]], own.at[pieces[part]], load_sem.at[part])

    def load_table(quarter):
        return pltpu.make_async_copy(table_hbm.at[core, quarter], table.at[quarter], table_sem.at[quarter])

    load(0).start()
    for quarter in range(CHUNKS):
        load_table(quarter).start()
    load(1).start()

    def device(to_y, to_xh, to_z, to_xl, to_core=core):
        return {"freq": (to_y * 2 + to_xh) * 2 + to_core, "row": to_z, "col": to_xl}

    sibling = device(y, xh, z, xl, 1 - core)
    partner = device(y, xh, z, 1 - xl)
    above, below = device(y, xh, up, xl), device(y, xh, down, xl)

    barrier = pltpu.get_barrier_semaphore()
    others = [sibling]
    others += [device(lax.rem(y + step, 4), xh, z, xl) for step in range(1, 4)]
    others += [device(lax.rem(y + step, 4), 1 - xh, z, 1 - xl) for step in range(4)]
    others += [partner, above, below]
    for one in others:
        pl.semaphore_signal(barrier, inc=1, device_id=one, device_id_type=MESH)
    pl.semaphore_wait(barrier, len(others))

    def remote(source, target, send, recv, where):
        return pltpu.make_async_remote_copy(
            src_ref=source, dst_ref=target, send_sem=send, recv_sem=recv, device_id=where, device_id_type=MESH
        )

    def swap(part):
        return remote(
            own_ref.at[pieces[part]], other.at[pieces[part]], core_send.at[part], core_recv.at[part], sibling
        )

    for part in range(2):
        swap(part).start()

    def spot(t):
        return lax.rem(t, CHUNKS), pl.ds(pl.multiple_of((t // CHUNKS) * HALF_SPEC, HALF_SPEC), HALF_SPEC)

    def home(t, side, from_y, from_xh):
        k, lanes = spot(t)
        return rows.at[k, :, side, from_y, from_xh, :, lanes]

    def first(t, step, flip):
        to_y, to_xh, to_xl = lax.rem(y + step, 4), (1 - xh if flip else xh), (1 - xl if flip else xl)
        index = flip * 4 + step
        return remote(
            made.at[t, to_y * 2 + to_xh], home(t, xl, y, xh),
            first_send.at[t, index], first_recv.at[t, index], device(to_y, to_xh, z, to_xl),
        )

    def first_arrival(t, step, flip):
        from_y, from_xh, from_xl = lax.rem(y + 4 - step, 4), (1 - xh if flip else xh), (1 - xl if flip else xl)
        index = flip * 4 + step
        place = home(t, from_xl, from_y, from_xh)
        return remote(
            place, place, first_send.at[t, index], first_recv.at[t, index], device(from_y, from_xh, z, from_xl)
        )

    def local(t):
        return pltpu.make_async_copy(made.at[t, y * 2 + xh], home(t, xl, y, xh), local_sem.at[t])

    def pair(t, part, mine=True):
        k, lanes = spot(t)
        side = xl if (part == 0) == mine else 1 - xl
        place = rows.at[k, :, side, :, xh if part == 0 else 1 - xh, :, lanes]
        return remote(place, place, pair_send.at[t, part], pair_recv.at[t, part], partner)

    def ring(t, part, way):
        k, lanes = spot(t)
        column = xh if part == 0 else 1 - xh
        return remote(
            rows.at[k, :, xl, :, column, :, lanes], planes.at[way, k, :, :, column, :, lanes],
            ring_send.at[t, part, way], ring_recv.at[t, part, way], above if way == 0 else below,
        )

    def onward(t, part):
        k, lanes = spot(t)
        column = xh if part == 0 else 1 - xh
        return remote(
            planes.at[part, k, :, :, column, :, lanes], planes.at[2, k, :, :, column, :, lanes],
            pass_send.at[t, part], pass_recv.at[t, part], above if part == 0 else below,
        )

    def fold(half):
        load(half).wait()
        filter_half(half, own, 0, weight_ref, frames, folded)
        swap(half).wait_recv()
        filter_half(half, other, 4, weight_ref, frames, folded)

    fold(0)
    for quarter in range(CHUNKS):
        load_table(quarter).wait()

    @pl.loop(0, STEPS + 3)
    def _(turn):
        @pl.when(turn == CHUNKS)
        def _():
            fold(1)

        @pl.when(turn < STEPS)
        def _():
            def write(target, value):
                made[turn, target] = value

            transform_chunk(turn // CHUNKS, lax.rem(turn, CHUNKS), core, table, folded, turned, write)
            local(turn).start()
            for step in range(1, 4):
                first(turn, step, 0).start()
            for step in range(4):
                first(turn, step, 1).start()

        @pl.when((turn >= 1) & (turn <= STEPS))
        def _():
            t = turn - 1
            local(t).wait()
            for step in range(1, 4):
                first_arrival(t, step, 0).wait_recv()
            for way in range(2):
                ring(t, 0, way).start()
            pair(t, 0).start()
            for step in range(4):
                first_arrival(t, step, 1).wait_recv()
            pair(t, 1).start()

        @pl.when((turn >= 2) & (turn <= STEPS + 1))
        def _():
            t = turn - 2
            pair(t, 1, False).wait_recv()
            for way in range(2):
                ring(t, 1, way).start()

        @pl.when(turn >= 3)
        def _():
            t = turn - 3
            for part in range(2):
                ring(t, part, part).wait_recv()
                onward(t, part).start()

    for part in range(2):
        swap(part).wait_send()

    @pl.loop(0, STEPS)
    def _(t):
        pair(t, 0, False).wait_recv()
        for part in range(2):
            ring(t, part, 1 - part).wait_recv()
            onward(t, part).wait_recv()
        for step in range(1, 4):
            first(t, step, 0).wait_send()
        for step in range(4):
            first(t, step, 1).wait_send()
        for part in range(2):
            pair(t, part).wait_send()
            for way in range(2):
                ring(t, part, way).wait_send()
            onward(t, part).wait_send()


def exchange(voltages, weights, table):
    any_space = pl.BlockSpec(memory_space=pl.ANY)
    dma = pltpu.SemaphoreType.DMA
    return pl.pallas_call(
        exchange_kernel,
        in_specs=[any_space, pl.BlockSpec(memory_space=pltpu.VMEM), any_space],
        out_specs=[any_space, any_space],
        out_shape=[
            jax.ShapeDtypeStruct((CHUNKS, 2 * CHUNK_CHAN, 2, 4, 2, 8, SPEC), BF16),
            jax.ShapeDtypeStruct((3, CHUNKS, 2 * CHUNK_CHAN, 4, 2, 8, SPEC), BF16),
        ],
        scratch_shapes=[
            pltpu.VMEM(voltages.shape, BF16),
            pltpu.VMEM(voltages.shape, BF16),
            pltpu.VMEM(table.shape[1:], BF16),
            pltpu.VMEM((2, 4 * 132, 128), F32),
            pltpu.VMEM((2, 2, 2, 4, 2 * HALF_SPEC, HALF), BF16),
            pltpu.VMEM((TARGETS * CHUNK_CHAN * 16, 128), F32),
            pltpu.VMEM((STEPS, TARGETS, 2 * CHUNK_CHAN, 8, HALF_SPEC), BF16),
            dma((2,)),
            dma((CHUNKS,)),
            dma((2,)),
            dma((2,)),
            dma((STEPS,)),
            dma((STEPS, 8)),
            dma((STEPS, 8)),
            dma((STEPS, 2)),
            dma((STEPS, 2)),
            dma((STEPS, 2, 2)),
            dma((STEPS, 2, 2)),
            dma((STEPS, 2)),
            dma((STEPS, 2)),
        ],
        compiler_params=pltpu.CompilerParams(collective_id=0, has_side_effects=True, vmem_limit_bytes=56 << 20),
        name="exchange",
    )(voltages, weights, table)


def correlate_kernel(place_ref, rows_hbm, planes_hbm, out_hbm, rows_ref, planes_ref, out_ref, rows_sem, planes_sem, out_sem):
    z, xl = place_ref[0], place_ref[1]

    def channels(g):
        return pl.ds(g * STEP_CHAN, STEP_CHAN)

    def load_rows(g):
        return pltpu.make_async_copy(rows_hbm.at[channels(g)], rows_ref.at[channels(g)], rows_sem.at[g])

    def load_planes(g):
        return pltpu.make_async_copy(planes_hbm.at[:, channels(g)], planes_ref.at[:, channels(g)], planes_sem.at[g])

    def store(g):
        return pltpu.make_async_copy(out_ref.at[channels(g)], out_hbm.at[channels(g)], out_sem.at[g])

    groups = LOCAL_CHAN // STEP_CHAN

    @pl.loop(0, groups)
    def _(g):
        load_rows(g).start()
        load_planes(g).start()

    @pl.loop(0, groups)
    def _(g):
        load_rows(g).wait()
        load_planes(g).wait()
        for index in range(STEP_CHAN):
            c = g * STEP_CHAN + index
            real, imag = rows_ref[c, 0], rows_ref[c, 1]
            weights = jnp.concatenate(
                [jnp.concatenate([real, imag], axis=1), jnp.concatenate([imag, -real], axis=1)], axis=0
            )
            start = pl.multiple_of(xl * 64, 64)
            parts = []
            for part in range(2):
                pieces = [rows_ref[c, part, pl.ds(start, 64)]]
                pieces += [planes_ref[slot, c, part] for slot in range(3)]
                parts.append(jnp.concatenate(pieces, axis=0))
            value = lax.dot_general(
                jnp.concatenate(parts, axis=1), weights, (((1,), (1,)), ((), ())), preferred_element_type=F32
            )
            value = value * (1.0 / SPEC)
            for index, shift in enumerate((0, 3, 1, 2)):
                plane = lax.rem(z + shift, 4)
                out_ref[c, 0, plane] = value[index * 64 : index * 64 + 64, :128]
                out_ref[c, 1, plane] = value[index * 64 : index * 64 + 64, 128:]
        store(g).start()

    @pl.loop(0, groups)
    def _(g):
        store(g).wait()


def correlate(rows, planes, place):
    any_space = pl.BlockSpec(memory_space=pl.ANY)
    groups = LOCAL_CHAN // STEP_CHAN
    return pl.pallas_call(
        correlate_kernel,
        in_specs=[pl.BlockSpec(memory_space=pltpu.SMEM), any_space, any_space],
        out_specs=any_space,
        out_shape=jax.ShapeDtypeStruct((LOCAL_CHAN, 2, 4, 64, 128), F32),
        scratch_shapes=[
            pltpu.VMEM(rows.shape, BF16),
            pltpu.VMEM(planes.shape, BF16),
            pltpu.VMEM((LOCAL_CHAN, 2, 4, 64, 128), F32),
            pltpu.SemaphoreType.DMA((groups,)),
            pltpu.SemaphoreType.DMA((groups,)),
            pltpu.SemaphoreType.DMA((groups,)),
        ],
        compiler_params=pltpu.CompilerParams(vmem_limit_bytes=58 << 20),
        name="correlate",
    )(place, rows, planes)


def shards(table, voltages, tap_table):
    z, xl = lax.axis_index("row"), lax.axis_index("col")
    weights = tap_table.astype(F32)
    rows, planes = exchange(jnp.transpose(voltages, (1, 0, 2)), weights, table)
    rows = rows.reshape(LOCAL_CHAN, 2, 128, SPEC)
    planes = planes.reshape(3, LOCAL_CHAN, 2, 64, SPEC)
    return correlate(rows, planes, jnp.stack([z, xl]).astype(jnp.int32))


def solution(mesh):
    table = dft_tables()

    def run(voltages, tap_table):
        return jax.shard_map(
            shards,
            mesh=mesh,
            in_specs=(P(), P(("row", "col", "freq"), None, None), P()),
            out_specs=P("freq", None, None, "col", "row"),
            check_vma=False,
        )(jnp.asarray(table), voltages, tap_table)

    return run
```

```python
import math

import jax
import jax.numpy as jnp
import ml_dtypes
import numpy as np
from jax import lax
from jax.experimental import pallas as pl
from jax.experimental.pallas import tpu as pltpu
from jax.sharding import PartitionSpec as P

NFFT = 2048
HALF = NFFT // 2
TAPS = 4
SPEC = 256
CHAN = 1024
GROUPS = 16
LOCAL_CHAN = CHAN // GROUPS
CHUNKS = 4
CHUNK_CHAN = LOCAL_CHAN // CHUNKS
FOLD_CHAN = CHUNK_CHAN // 2
TARGETS = 8
ROWS = 2 * TARGETS * FOLD_CHAN
HALF_SPEC = SPEC // 2
STEPS = 2 * CHUNKS
STEP_CHAN = 4
F32 = jnp.float32
BF16 = jnp.bfloat16
MESH = pl.DeviceIdType.MESH


def dft_tables():
    core, chunk, parity, part, target, index = np.meshgrid(
        np.arange(2), np.arange(CHUNKS), np.arange(2), np.arange(2), np.arange(TARGETS), np.arange(FOLD_CHAN),
        indexing="ij",
    )
    channel = (target * 2 + core) * LOCAL_CHAN + chunk * CHUNK_CHAN + 2 * index + parity
    phase = (channel[..., None] * np.arange(HALF)) % NFFT
    angle = phase * (2.0 * np.pi / NFFT)
    cosine = np.where(phase % (NFFT // 2) == NFFT // 4, 0.0, np.cos(angle))
    sine = np.where(phase % (NFFT // 2) == 0, 0.0, np.sin(angle))
    values = np.where(part[..., None] == 0, cosine, -sine) / (64.0 * math.sqrt(NFFT) * 4096.0)
    high = values.astype(ml_dtypes.bfloat16)
    low = (values - high.astype(np.float64)).astype(ml_dtypes.bfloat16)
    shape = (2, CHUNKS, 2, ROWS, HALF)
    return np.concatenate([high.reshape(shape), low.reshape(shape)], axis=3)


def filter_half(half, source, first, weight_ref, frames, folded):
    count = HALF_SPEC + TAPS - 1

    @pl.loop(0, HALF // 128)
    def _(step):
        low = pl.multiple_of(step * 128, 128)
        columns = (low, pl.multiple_of(low + HALF, 128))
        for side in range(2):
            block = source[pl.ds(half * HALF_SPEC, count), :, pl.ds(columns[side], 128)]
            frames[side, 0 : 4 * count, :] = block.astype(F32).reshape(4 * count, 128)
        for row in range(4):
            slot = first + row
            for start in range(0, HALF_SPEC, 64):
                sides = []
                for side in range(2):
                    total = None
                    for tap in range(TAPS):
                        weight = weight_ref[pl.ds(tap, 1), pl.ds(columns[side], 128)]
                        term = weight * frames[side, pl.ds((start + tap) * 4 + row, 64, stride=4), :]
                        total = term if total is None else total + term
                    sides.append(total)
                place = (slot % 2) * HALF_SPEC + start
                for parity, value in ((0, sides[0] + sides[1]), (1, sides[0] - sides[1])):
                    top = value.astype(BF16)
                    rest = (value - top.astype(F32)).astype(BF16)
                    folded[parity, 0, half, slot // 2, place : place + 64, pl.ds(low, 128)] = top
                    folded[parity, 1, half, slot // 2, place : place + 64, pl.ds(low, 128)] = rest


def transform_chunk(half, quarter, core, table_ref, folded, turned, write):
    contract = (((1,), (1,)), ((), ()))

    @pl.loop(0, 4)
    def _(duo):
        for parity in range(2):
            top = folded[parity, 0, half, duo]
            both = lax.dot_general(table_ref[quarter, parity], top, contract, preferred_element_type=F32)
            rest = lax.dot_general(
                table_ref[quarter, parity, :ROWS], folded[parity, 1, half, duo], contract, preferred_element_type=F32
            )
            value = both[:ROWS] + both[ROWS:] + rest
            for sub in range(2):
                row = lax.rem(2 * duo + sub + 4 * core, 8)
                for part in range(2):
                    turned[pl.ds(parity * 16 + part * 8 + row, ROWS // 2, stride=32), :] = value[
                        part * (ROWS // 2) : (part + 1) * (ROWS // 2), sub * 128 : sub * 128 + 128
                    ]

    block = CHUNK_CHAN * 16

    @pl.loop(0, TARGETS)
    def _(target):
        rows = turned[pl.ds(pl.multiple_of(target * block, block), block), :]
        write(target, rows.reshape(2 * CHUNK_CHAN, 8, 128).astype(BF16))


def stacked(real, imag):
    return jnp.concatenate([jnp.concatenate([real, imag], axis=1), jnp.concatenate([imag, -real], axis=1)], axis=0)


def exchange_kernel(
    own_ref, weight_ref, table_hbm, rows, near, far, crossed,
    own, other, table, frames, folded, turned, made, rows_part, near_part, products,
    load_sem, table_sem, core_send, core_recv,
    local_sem, first_send, first_recv, pair_send, pair_recv, ring_send, ring_recv, pass_send, pass_recv,
    part_sem, back_send, back_recv,
):
    freq, z, xl = lax.axis_index("freq"), lax.axis_index("row"), lax.axis_index("col")
    core = lax.rem(freq, 2)
    xh = lax.rem(freq // 2, 2)
    y = freq // 4
    up, down = lax.rem(z + 1, 4), lax.rem(z + 3, 4)
    pieces = (pl.ds(0, HALF_SPEC + TAPS - 1), pl.ds(HALF_SPEC + TAPS - 1, HALF_SPEC))

    def load(part):
        return pltpu.make_async_copy(own_ref.at[pieces[part]], own.at[pieces[part]], load_sem.at[part])

    def load_table(quarter):
        return pltpu.make_async_copy(table_hbm.at[core, quarter], table.at[quarter], table_sem.at[quarter])

    load(0).start()
    for quarter in range(CHUNKS):
        load_table(quarter).start()
    load(1).start()

    def device(to_y, to_xh, to_z, to_xl, to_core=core):
        return {"freq": (to_y * 2 + to_xh) * 2 + to_core, "row": to_z, "col": to_xl}

    sibling = device(y, xh, z, xl, 1 - core)
    partner = device(y, xh, z, 1 - xl)
    above, below = device(y, xh, up, xl), device(y, xh, down, xl)

    barrier = pltpu.get_barrier_semaphore()
    others = [sibling]
    others += [device(lax.rem(y + step, 4), xh, z, xl) for step in range(1, 4)]
    others += [device(lax.rem(y + step, 4), 1 - xh, z, 1 - xl) for step in range(4)]
    others += [partner, above, below, device(y, xh, up, 1 - xl), device(y, xh, down, 1 - xl)]
    for one in others:
        pl.semaphore_signal(barrier, inc=1, device_id=one, device_id_type=MESH)
    pl.semaphore_wait(barrier, len(others))

    def remote(source, target, send, recv, where):
        return pltpu.make_async_remote_copy(
            src_ref=source, dst_ref=target, send_sem=send, recv_sem=recv, device_id=where, device_id_type=MESH
        )

    def swap(part):
        return remote(
            own_ref.at[pieces[part]], other.at[pieces[part]], core_send.at[part], core_recv.at[part], sibling
        )

    for part in range(2):
        swap(part).start()

    def spot(t):
        return t // 2, pl.ds(pl.multiple_of(lax.rem(t, 2) * HALF_SPEC, HALF_SPEC), HALF_SPEC)

    def home(t, side, from_y, from_xh):
        k, lanes = spot(t)
        return rows.at[k, :, side, from_y, from_xh, :, lanes]

    def first(t, step, flip):
        to_y, to_xh, to_xl = lax.rem(y + step, 4), (1 - xh if flip else xh), (1 - xl if flip else xl)
        index = flip * 4 + step
        return remote(
            made.at[t, to_y * 2 + to_xh], home(t, xl, y, xh),
            first_send.at[t, index], first_recv.at[t, index], device(to_y, to_xh, z, to_xl),
        )

    def first_arrival(t, step, flip):
        from_y, from_xh, from_xl = lax.rem(y + 4 - step, 4), (1 - xh if flip else xh), (1 - xl if flip else xl)
        index = flip * 4 + step
        place = home(t, from_xl, from_y, from_xh)
        return remote(
            place, place, first_send.at[t, index], first_recv.at[t, index], device(from_y, from_xh, z, from_xl)
        )

    def local(t):
        return pltpu.make_async_copy(made.at[t, y * 2 + xh], home(t, xl, y, xh), local_sem.at[t])

    def pair(t, part, mine=True):
        k, lanes = spot(t)
        side = xl if (part == 0) == mine else 1 - xl
        place = rows.at[k, :, side, :, xh if part == 0 else 1 - xh, :, lanes]
        return remote(place, place, pair_send.at[t, part], pair_recv.at[t, part], partner)

    def ring(t, part, way):
        k, lanes = spot(t)
        column = xh if part == 0 else 1 - xh
        share = pl.ds(way * CHUNK_CHAN, CHUNK_CHAN)
        return remote(
            rows.at[k, share, xl, :, column, :, lanes], near.at[k, share, :, column, :, lanes],
            ring_send.at[t, part, way], ring_recv.at[t, part, way], above if way == 0 else below,
        )

    def onward(t, part, way):
        k, lanes = spot(t)
        column = xh if part == 0 else 1 - xh
        share = pl.ds(way * CHUNK_CHAN, CHUNK_CHAN)
        return remote(
            near.at[k, share, :, column, :, lanes], far.at[k, share, :, column, :, lanes],
            pass_send.at[t, part, way], pass_recv.at[t, part, way], above if way == 0 else below,
        )

    def back(k, way, side):
        share = pl.ds(way * FOLD_CHAN, FOLD_CHAN)
        return remote(
            products.at[k, side, share], crossed.at[xl, k, share],
            back_send.at[k, way, side], back_recv.at[k, way, xl],
            device(y, xh, down if way == 0 else up, side),
        )

    def back_arrival(k, way, side):
        share = pl.ds(way * FOLD_CHAN, FOLD_CHAN)
        place = crossed.at[side, k, share]
        return remote(
            place, place, back_send.at[k, way, side], back_recv.at[k, way, side],
            device(y, xh, up if way == 0 else down, side),
        )

    def multiply(k):
        copies = [
            pltpu.make_async_copy(rows.at[k], rows_part, part_sem.at[0]),
            pltpu.make_async_copy(near.at[k], near_part, part_sem.at[1]),
        ]
        for copy in copies:
            copy.start()
        for copy in copies:
            copy.wait()

        @pl.loop(0, CHUNK_CHAN)
        def _(c):
            left = [rows_part[2 * c + part].reshape(128, SPEC) for part in range(2)]
            right = [near_part[2 * c + part].reshape(64, SPEC) for part in range(2)]
            value = lax.dot_general(
                jnp.concatenate(left, axis=1), stacked(right[0], right[1]), (((1,), (1,)), ((), ())),
                preferred_element_type=F32,
            )
            value = (value * (1.0 / SPEC)).astype(BF16)
            products[k, 0, c] = value[:64]
            products[k, 1, c] = value[64:]

        for way in range(2):
            for side in range(2):
                back(k, way, side).start()

    def fold(half):
        load(half).wait()
        filter_half(half, own, 0, weight_ref, frames, folded)
        swap(half).wait_recv()
        filter_half(half, other, 4, weight_ref, frames, folded)

    fold(0)
    for quarter in range(CHUNKS):
        load_table(quarter).wait()

    @pl.loop(0, STEPS + 4)
    def _(turn):
        @pl.when(turn == 1)
        def _():
            fold(1)

        @pl.when(turn < STEPS)
        def _():
            def write(target, value):
                made[turn, target] = value

            transform_chunk(lax.rem(turn, 2), turn // 2, core, table, folded, turned, write)
            local(turn).start()
            for step in range(1, 4):
                first(turn, step, 0).start()
            for step in range(4):
                first(turn, step, 1).start()

        @pl.when((turn >= 1) & (turn <= STEPS))
        def _():
            t = turn - 1
            local(t).wait()
            for step in range(1, 4):
                first_arrival(t, step, 0).wait_recv()
            for way in range(2):
                ring(t, 0, way).start()
            pair(t, 0).start()
            for step in range(4):
                first_arrival(t, step, 1).wait_recv()
            pair(t, 1).start()

        @pl.when((turn >= 2) & (turn <= STEPS + 1))
        def _():
            t = turn - 2
            pair(t, 1, False).wait_recv()
            for way in range(2):
                ring(t, 1, way).start()

        @pl.when((turn >= 3) & (turn <= STEPS + 2))
        def _():
            t = turn - 3
            for part in range(2):
                for way in range(2):
                    ring(t, part, way).wait_recv()
                    onward(t, part, way).start()
            pair(t, 0, False).wait_recv()

        @pl.when((turn >= 5) & (lax.rem(turn, 2) == 1))
        def _():
            multiply((turn - 5) // 2)

    for part in range(2):
        swap(part).wait_send()

    @pl.loop(0, CHUNKS)
    def _(k):
        for way in range(2):
            for side in range(2):
                back_arrival(k, way, side).wait_recv()
                back(k, way, side).wait_send()

    @pl.loop(0, STEPS)
    def _(t):
        for step in range(1, 4):
            first(t, step, 0).wait_send()
        for step in range(4):
            first(t, step, 1).wait_send()
        for part in range(2):
            pair(t, part).wait_send()
            for way in range(2):
                ring(t, part, way).wait_send()
                onward(t, part, way).wait_recv()
                onward(t, part, way).wait_send()


def exchange(voltages, weights, table):
    any_space = pl.BlockSpec(memory_space=pl.ANY)
    dma = pltpu.SemaphoreType.DMA
    return pl.pallas_call(
        exchange_kernel,
        in_specs=[any_space, pl.BlockSpec(memory_space=pltpu.VMEM), any_space],
        out_specs=[any_space] * 4,
        out_shape=[
            jax.ShapeDtypeStruct((CHUNKS, 2 * CHUNK_CHAN, 2, 4, 2, 8, SPEC), BF16),
            jax.ShapeDtypeStruct((CHUNKS, 2 * CHUNK_CHAN, 4, 2, 8, SPEC), BF16),
            jax.ShapeDtypeStruct((CHUNKS, 2 * CHUNK_CHAN, 4, 2, 8, SPEC), BF16),
            jax.ShapeDtypeStruct((2, CHUNKS, CHUNK_CHAN, 64, 128), BF16),
        ],
        scratch_shapes=[
            pltpu.VMEM(voltages.shape, BF16),
            pltpu.VMEM(voltages.shape, BF16),
            pltpu.VMEM(table.shape[1:], BF16),
            pltpu.VMEM((2, 4 * 132, 128), F32),
            pltpu.VMEM((2, 2, 2, 4, 2 * HALF_SPEC, HALF), BF16),
            pltpu.VMEM((TARGETS * CHUNK_CHAN * 16, 128), F32),
            pltpu.VMEM((STEPS, TARGETS, 2 * CHUNK_CHAN, 8, HALF_SPEC), BF16),
            pltpu.VMEM((2 * CHUNK_CHAN, 2, 4, 2, 8, SPEC), BF16),
            pltpu.VMEM((2 * CHUNK_CHAN, 4, 2, 8, SPEC), BF16),
            pltpu.VMEM((CHUNKS, 2, CHUNK_CHAN, 64, 128), BF16),
            dma((2,)),
            dma((CHUNKS,)),
            dma((2,)),
            dma((2,)),
            dma((STEPS,)),
            dma((STEPS, 8)),
            dma((STEPS, 8)),
            dma((STEPS, 2)),
            dma((STEPS, 2)),
            dma((STEPS, 2, 2)),
            dma((STEPS, 2, 2)),
            dma((STEPS, 2, 2)),
            dma((STEPS, 2, 2)),
            dma((2,)),
            dma((CHUNKS, 2, 2)),
            dma((CHUNKS, 2, 2)),
        ],
        compiler_params=pltpu.CompilerParams(collective_id=0, has_side_effects=True, vmem_limit_bytes=56 << 20),
        name="exchange",
    )(voltages, weights, table)


def correlate_kernel(
    place_ref, rows_hbm, near_hbm, far_hbm, crossed_hbm, out_hbm,
    rows_ref, near_ref, far_ref, crossed_ref, out_ref, load_sem, out_sem,
):
    z, xl = place_ref[0], place_ref[1]

    def channels(g):
        return pl.ds(g * STEP_CHAN, STEP_CHAN)

    def loads(g):
        some = channels(g)
        pairs = [(rows_hbm.at[some], rows_ref.at[some]), (near_hbm.at[some], near_ref.at[some])]
        pairs += [(far_hbm.at[some], far_ref.at[some]), (crossed_hbm.at[:, some], crossed_ref.at[:, some])]
        return [pltpu.make_async_copy(a, b, load_sem.at[g, i]) for i, (a, b) in enumerate(pairs)]

    def store(g):
        return pltpu.make_async_copy(out_ref.at[channels(g)], out_hbm.at[channels(g)], out_sem.at[g])

    groups = LOCAL_CHAN // STEP_CHAN

    @pl.loop(0, groups)
    def _(g):
        for copy in loads(g):
            copy.start()

    @pl.loop(0, groups)
    def _(g):
        for copy in loads(g):
            copy.wait()
        down_share = lax.rem(g // (FOLD_CHAN // STEP_CHAN), 2)
        near_plane = lax.rem(z + 3 + 2 * down_share, 4)
        far_plane = lax.rem(z + 2, 4)
        crossed_plane = lax.rem(z + 1 + 2 * down_share, 4)
        for index in range(STEP_CHAN):
            c = g * STEP_CHAN + index
            start = pl.multiple_of(xl * 64, 64)
            parts = []
            for part in range(2):
                pieces = [rows_ref[c, part, pl.ds(start, 64)], near_ref[c, part], far_ref[c, part]]
                parts.append(jnp.concatenate(pieces, axis=0))
            value = lax.dot_general(
                jnp.concatenate(parts, axis=1), stacked(rows_ref[c, 0], rows_ref[c, 1]), (((1,), (1,)), ((), ())),
                preferred_element_type=F32,
            )
            value = value * (1.0 / SPEC)
            for index, plane in enumerate((z, near_plane, far_plane)):
                out_ref[c, 0, plane] = value[index * 64 : index * 64 + 64, :128]
                out_ref[c, 1, plane] = value[index * 64 : index * 64 + 64, 128:]
            sides = [crossed_ref[side, c].astype(F32) for side in range(2)]
            out_ref[c, 0, crossed_plane] = jnp.concatenate([side[:, :64] for side in sides], axis=1)
            out_ref[c, 1, crossed_plane] = jnp.concatenate([side[:, 64:] for side in sides], axis=1)
        store(g).start()

    @pl.loop(0, groups)
    def _(g):
        store(g).wait()


def correlate(rows, near, far, crossed, place):
    any_space = pl.BlockSpec(memory_space=pl.ANY)
    groups = LOCAL_CHAN // STEP_CHAN
    return pl.pallas_call(
        correlate_kernel,
        in_specs=[pl.BlockSpec(memory_space=pltpu.SMEM)] + [any_space] * 4,
        out_specs=any_space,
        out_shape=jax.ShapeDtypeStruct((LOCAL_CHAN, 2, 4, 64, 128), F32),
        scratch_shapes=[
            pltpu.VMEM(rows.shape, BF16),
            pltpu.VMEM(near.shape, BF16),
            pltpu.VMEM(far.shape, BF16),
            pltpu.VMEM(crossed.shape, BF16),
            pltpu.VMEM((LOCAL_CHAN, 2, 4, 64, 128), F32),
            pltpu.SemaphoreType.DMA((groups, 4)),
            pltpu.SemaphoreType.DMA((groups,)),
        ],
        compiler_params=pltpu.CompilerParams(vmem_limit_bytes=58 << 20),
        name="correlate",
    )(place, rows, near, far, crossed)


def shards(table, voltages, tap_table):
    z, xl = lax.axis_index("row"), lax.axis_index("col")
    weights = tap_table.astype(F32)
    rows, near, far, crossed = exchange(jnp.transpose(voltages, (1, 0, 2)), weights, table)
    rows = rows.reshape(LOCAL_CHAN, 2, 128, SPEC)
    near = near.reshape(LOCAL_CHAN, 2, 64, SPEC)
    far = far.reshape(LOCAL_CHAN, 2, 64, SPEC)
    crossed = crossed.reshape(2, LOCAL_CHAN, 64, 128)
    return correlate(rows, near, far, crossed, jnp.stack([z, xl]).astype(jnp.int32))


def solution(mesh):
    table = dft_tables()

    def run(voltages, tap_table):
        return jax.shard_map(
            shards,
            mesh=mesh,
            in_specs=(P(), P(("row", "col", "freq"), None, None), P()),
            out_specs=P("freq", None, None, "col", "row"),
            check_vma=False,
        )(jnp.asarray(table), voltages, tap_table)

    return run
```

```python
import math

import jax
import jax.numpy as jnp
import ml_dtypes
import numpy as np
from jax import lax
from jax.experimental import pallas as pl
from jax.experimental.pallas import tpu as pltpu
from jax.sharding import PartitionSpec as P

NFFT = 2048
HALF = NFFT // 2
TAPS = 4
SPEC = 256
CHAN = 1024
GROUPS = 16
LOCAL_CHAN = CHAN // GROUPS
CHUNKS = 4
CHUNK_CHAN = LOCAL_CHAN // CHUNKS
FOLD_CHAN = CHUNK_CHAN // 2
TARGETS = 8
ROWS = 2 * TARGETS * FOLD_CHAN
HALF_SPEC = SPEC // 2
STEPS = 2 * CHUNKS
STEP_CHAN = 4
PAIR_LAG = 2
PASS_LAG = 3
BACK_LAG = 4
F32 = jnp.float32
BF16 = jnp.bfloat16
MESH = pl.DeviceIdType.MESH


def dft_tables():
    core, chunk, parity, part, target, index = np.meshgrid(
        np.arange(2), np.arange(CHUNKS), np.arange(2), np.arange(2), np.arange(TARGETS), np.arange(FOLD_CHAN),
        indexing="ij",
    )
    channel = (target * 2 + core) * LOCAL_CHAN + chunk * CHUNK_CHAN + 2 * index + parity
    phase = (channel[..., None] * np.arange(HALF)) % NFFT
    angle = phase * (2.0 * np.pi / NFFT)
    cosine = np.where(phase % (NFFT // 2) == NFFT // 4, 0.0, np.cos(angle))
    sine = np.where(phase % (NFFT // 2) == 0, 0.0, np.sin(angle))
    values = np.where(part[..., None] == 0, cosine, -sine) / (64.0 * math.sqrt(NFFT) * 4096.0)
    high = values.astype(ml_dtypes.bfloat16)
    low = (values - high.astype(np.float64)).astype(ml_dtypes.bfloat16)
    shape = (2, CHUNKS, 2, ROWS, HALF)
    return np.concatenate([high.reshape(shape), low.reshape(shape)], axis=3)


def filter_half(half, source, first, taps_ref, frames, mixed, folded):
    count = 4 * (HALF_SPEC + TAPS - 1)

    @pl.loop(0, HALF // 128)
    def _(step):
        low = pl.multiple_of(step * 128, 128)
        columns = (low, pl.multiple_of(low + HALF, 128))
        weights = []
        for side in range(2):
            block = source[pl.ds(half * HALF_SPEC, HALF_SPEC + TAPS - 1), :, pl.ds(columns[side], 128)]
            frames[side, 0:count, :] = block.astype(F32).reshape(count, 128)
            weights.append([taps_ref[pl.ds(tap, 1), pl.ds(columns[side], 128)].astype(F32) for tap in range(TAPS)])
        for start in range(0, 4 * HALF_SPEC, 64):
            sides = []
            for side in range(2):
                even = frames[side, start : start + 72, :]
                odd = frames[side, start + 4 : start + 76, :]
                w = weights[side]
                sides.append(w[0] * even[:64] + w[1] * odd[:64] + w[2] * even[8:] + w[3] * odd[8:])
            mixed[0, start : start + 64, :] = sides[0] + sides[1]
            mixed[1, start : start + 64, :] = sides[0] - sides[1]
        for row in range(4):
            slot = first + row
            place = (slot % 2) * HALF_SPEC
            for parity in range(2):
                value = mixed[parity, pl.ds(row, HALF_SPEC, stride=4), :]
                top = value.astype(BF16)
                rest = (value - top.astype(F32)).astype(BF16)
                folded[parity, 0, half, slot // 2, place : place + HALF_SPEC, pl.ds(low, 128)] = top
                folded[parity, 1, half, slot // 2, place : place + HALF_SPEC, pl.ds(low, 128)] = rest


def transform_chunk(half, quarter, core, table_ref, folded, turned, write):
    contract = (((1,), (1,)), ((), ()))

    @pl.loop(0, 4)
    def _(duo):
        for parity in range(2):
            top = folded[parity, 0, half, duo]
            both = lax.dot_general(table_ref[quarter, parity], top, contract, preferred_element_type=F32)
            rest = lax.dot_general(
                table_ref[quarter, parity, :ROWS], folded[parity, 1, half, duo], contract, preferred_element_type=F32
            )
            value = both[:ROWS] + both[ROWS:] + rest
            for sub in range(2):
                row = lax.rem(2 * duo + sub + 4 * core, 8)
                for part in range(2):
                    turned[pl.ds(parity * 16 + part * 8 + row, ROWS // 2, stride=32), :] = value[
                        part * (ROWS // 2) : (part + 1) * (ROWS // 2), sub * 128 : sub * 128 + 128
                    ]

    block = CHUNK_CHAN * 16

    @pl.loop(0, TARGETS)
    def _(target):
        rows = turned[pl.ds(pl.multiple_of(target * block, block), block), :]
        write(target, rows.reshape(2 * CHUNK_CHAN, 8, 128).astype(BF16))


def stacked(real, imag):
    return jnp.concatenate([jnp.concatenate([real, imag], axis=1), jnp.concatenate([imag, -real], axis=1)], axis=0)


def exchange_kernel(
    own_ref, taps_ref, table_hbm, rows, near, far, crossed,
    own, other, table, frames, mixed, folded, turned, made, rows_part, near_part, products,
    load_sem, table_sem, core_send, core_recv,
    local_sem, first_send, first_recv, pair_send, pair_recv, ring_send, ring_recv, pass_send, pass_recv,
    part_sem, back_send, back_recv,
):
    freq, z, xl = lax.axis_index("freq"), lax.axis_index("row"), lax.axis_index("col")
    core = lax.rem(freq, 2)
    xh = lax.rem(freq // 2, 2)
    y = freq // 4
    up, down = lax.rem(z + 1, 4), lax.rem(z + 3, 4)
    pieces = (pl.ds(0, HALF_SPEC + TAPS - 1), pl.ds(HALF_SPEC + TAPS - 1, HALF_SPEC))

    def load(part):
        return pltpu.make_async_copy(own_ref.at[pieces[part]], own.at[pieces[part]], load_sem.at[part])

    def load_table(quarter):
        return pltpu.make_async_copy(table_hbm.at[core, quarter], table.at[quarter], table_sem.at[quarter])

    load(0).start()
    for quarter in range(CHUNKS):
        load_table(quarter).start()
    load(1).start()

    def device(to_y, to_xh, to_z, to_xl, to_core=core):
        return {"freq": (to_y * 2 + to_xh) * 2 + to_core, "row": to_z, "col": to_xl}

    sibling = device(y, xh, z, xl, 1 - core)
    partner = device(y, xh, z, 1 - xl)
    above, below = device(y, xh, up, xl), device(y, xh, down, xl)

    barrier = pltpu.get_barrier_semaphore()
    others = [sibling]
    others += [device(lax.rem(y + step, 4), xh, z, xl) for step in range(1, 4)]
    others += [device(lax.rem(y + step, 4), 1 - xh, z, 1 - xl) for step in range(4)]
    others += [partner, above, below, device(y, xh, up, 1 - xl), device(y, xh, down, 1 - xl)]
    for one in others:
        pl.semaphore_signal(barrier, inc=1, device_id=one, device_id_type=MESH)
    pl.semaphore_wait(barrier, len(others))

    def remote(source, target, send, recv, where):
        return pltpu.make_async_remote_copy(
            src_ref=source, dst_ref=target, send_sem=send, recv_sem=recv, device_id=where, device_id_type=MESH
        )

    def swap(part):
        return remote(
            own_ref.at[pieces[part]], other.at[pieces[part]], core_send.at[part], core_recv.at[part], sibling
        )

    for part in range(2):
        swap(part).start()

    def spot(t):
        return lax.rem(t, CHUNKS), pl.ds(pl.multiple_of((t // CHUNKS) * HALF_SPEC, HALF_SPEC), HALF_SPEC)

    def home(t, side, from_y, from_xh):
        k, lanes = spot(t)
        return rows.at[k, :, side, from_y, from_xh, :, lanes]

    def first(t, step, flip):
        to_y, to_xh, to_xl = lax.rem(y + step, 4), (1 - xh if flip else xh), (1 - xl if flip else xl)
        index = flip * 4 + step
        return remote(
            made.at[t, to_y * 2 + to_xh], home(t, xl, y, xh),
            first_send.at[t, index], first_recv.at[t, index], device(to_y, to_xh, z, to_xl),
        )

    def first_arrival(t, step, flip):
        from_y, from_xh, from_xl = lax.rem(y + 4 - step, 4), (1 - xh if flip else xh), (1 - xl if flip else xl)
        index = flip * 4 + step
        place = home(t, from_xl, from_y, from_xh)
        return remote(
            place, place, first_send.at[t, index], first_recv.at[t, index], device(from_y, from_xh, z, from_xl)
        )

    def local(t):
        return pltpu.make_async_copy(made.at[t, y * 2 + xh], home(t, xl, y, xh), local_sem.at[t])

    def pair(t, part, mine=True):
        k, lanes = spot(t)
        side = xl if (part == 0) == mine else 1 - xl
        place = rows.at[k, :, side, :, xh if part == 0 else 1 - xh, :, lanes]
        return remote(place, place, pair_send.at[t, part], pair_recv.at[t, part], partner)

    def ring(t, part, way):
        k, lanes = spot(t)
        column = xh if part == 0 else 1 - xh
        share = pl.ds(way * CHUNK_CHAN, CHUNK_CHAN)
        return remote(
            rows.at[k, share, xl, :, column, :, lanes], near.at[k, share, :, column, :, lanes],
            ring_send.at[t, part, way], ring_recv.at[t, part, way], above if way == 0 else below,
        )

    def onward(t, part, way):
        k, lanes = spot(t)
        column = xh if part == 0 else 1 - xh
        share = pl.ds(way * CHUNK_CHAN, CHUNK_CHAN)
        return remote(
            near.at[k, share, :, column, :, lanes], far.at[k, share, :, column, :, lanes],
            pass_send.at[t, part, way], pass_recv.at[t, part, way], above if way == 0 else below,
        )

    def back(k, way, side):
        share = pl.ds(way * FOLD_CHAN, FOLD_CHAN)
        return remote(
            products.at[k, side, share], crossed.at[xl, k, share],
            back_send.at[k, way, side], back_recv.at[k, way, xl],
            device(y, xh, down if way == 0 else up, side),
        )

    def back_arrival(k, way, side):
        share = pl.ds(way * FOLD_CHAN, FOLD_CHAN)
        place = crossed.at[side, k, share]
        return remote(
            place, place, back_send.at[k, way, side], back_recv.at[k, way, side],
            device(y, xh, up if way == 0 else down, side),
        )

    def multiply(k):
        copies = [
            pltpu.make_async_copy(rows.at[k], rows_part, part_sem.at[0]),
            pltpu.make_async_copy(near.at[k], near_part, part_sem.at[1]),
        ]
        for copy in copies:
            copy.start()
        for copy in copies:
            copy.wait()

        @pl.loop(0, CHUNK_CHAN)
        def _(c):
            left = [rows_part[2 * c + part].reshape(128, SPEC) for part in range(2)]
            right = [near_part[2 * c + part].reshape(64, SPEC) for part in range(2)]
            value = lax.dot_general(
                jnp.concatenate(left, axis=1), stacked(right[0], right[1]), (((1,), (1,)), ((), ())),
                preferred_element_type=F32,
            )
            value = (value * (1.0 / SPEC)).astype(BF16)
            products[k, 0, c] = value[:64]
            products[k, 1, c] = value[64:]

        for way in range(2):
            for side in range(2):
                back(k, way, side).start()

    def fold(half):
        load(half).wait()
        filter_half(half, own, 0, taps_ref, frames, mixed, folded)
        swap(half).wait_recv()
        filter_half(half, other, 4, taps_ref, frames, mixed, folded)

    fold(0)
    for quarter in range(CHUNKS):
        load_table(quarter).wait()

    @pl.loop(0, STEPS + BACK_LAG)
    def _(turn):
        @pl.when(turn == CHUNKS)
        def _():
            fold(1)

        @pl.when(turn < STEPS)
        def _():
            def write(target, value):
                made[turn, target] = value

            transform_chunk(turn // CHUNKS, lax.rem(turn, CHUNKS), core, table, folded, turned, write)
            local(turn).start()
            for step in range(1, 4):
                first(turn, step, 0).start()
            for step in range(4):
                first(turn, step, 1).start()

        @pl.when((turn >= 1) & (turn <= STEPS))
        def _():
            t = turn - 1
            local(t).wait()
            for step in range(1, 4):
                first_arrival(t, step, 0).wait_recv()
            for way in range(2):
                ring(t, 0, way).start()
            for step in range(4):
                first_arrival(t, step, 1).wait_recv()
            pair(t, 1).start()
            pair(t, 0).start()

        @pl.when((turn >= PAIR_LAG) & (turn < STEPS + PAIR_LAG))
        def _():
            t = turn - PAIR_LAG
            pair(t, 1, False).wait_recv()
            for way in range(2):
                ring(t, 1, way).start()

        @pl.when((turn >= PASS_LAG) & (turn < STEPS + PASS_LAG))
        def _():
            t = turn - PASS_LAG
            for part in range(2):
                for way in range(2):
                    ring(t, part, way).wait_recv()
                    onward(t, part, way).start()
            pair(t, 0, False).wait_recv()

        @pl.when(turn >= CHUNKS + BACK_LAG)
        def _():
            multiply(turn - CHUNKS - BACK_LAG)

    for part in range(2):
        swap(part).wait_send()

    @pl.loop(0, CHUNKS)
    def _(k):
        for way in range(2):
            for side in range(2):
                back_arrival(k, way, side).wait_recv()
                back(k, way, side).wait_send()

    @pl.loop(0, STEPS)
    def _(t):
        for step in range(1, 4):
            first(t, step, 0).wait_send()
        for step in range(4):
            first(t, step, 1).wait_send()
        for part in range(2):
            pair(t, part).wait_send()
            for way in range(2):
                ring(t, part, way).wait_send()
                onward(t, part, way).wait_recv()
                onward(t, part, way).wait_send()


def exchange(voltages, taps, table):
    any_space = pl.BlockSpec(memory_space=pl.ANY)
    dma = pltpu.SemaphoreType.DMA
    return pl.pallas_call(
        exchange_kernel,
        in_specs=[any_space, pl.BlockSpec(memory_space=pltpu.VMEM), any_space],
        out_specs=[any_space] * 4,
        out_shape=[
            jax.ShapeDtypeStruct((CHUNKS, 2 * CHUNK_CHAN, 2, 4, 2, 8, SPEC), BF16),
            jax.ShapeDtypeStruct((CHUNKS, 2 * CHUNK_CHAN, 4, 2, 8, SPEC), BF16),
            jax.ShapeDtypeStruct((CHUNKS, 2 * CHUNK_CHAN, 4, 2, 8, SPEC), BF16),
            jax.ShapeDtypeStruct((2, CHUNKS, CHUNK_CHAN, 64, 128), BF16),
        ],
        scratch_shapes=[
            pltpu.VMEM(voltages.shape, BF16),
            pltpu.VMEM(voltages.shape, BF16),
            pltpu.VMEM(table.shape[1:], BF16),
            pltpu.VMEM((2, 4 * 132, 128), F32),
            pltpu.VMEM((2, 4 * HALF_SPEC, 128), F32),
            pltpu.VMEM((2, 2, 2, 4, 2 * HALF_SPEC, HALF), BF16),
            pltpu.VMEM((TARGETS * CHUNK_CHAN * 16, 128), F32),
            pltpu.VMEM((STEPS, TARGETS, 2 * CHUNK_CHAN, 8, HALF_SPEC), BF16),
            pltpu.VMEM((2 * CHUNK_CHAN, 2, 4, 2, 8, SPEC), BF16),
            pltpu.VMEM((2 * CHUNK_CHAN, 4, 2, 8, SPEC), BF16),
            pltpu.VMEM((CHUNKS, 2, CHUNK_CHAN, 64, 128), BF16),
            dma((2,)),
            dma((CHUNKS,)),
            dma((2,)),
            dma((2,)),
            dma((STEPS,)),
            dma((STEPS, 8)),
            dma((STEPS, 8)),
            dma((STEPS, 2)),
            dma((STEPS, 2)),
            dma((STEPS, 2, 2)),
            dma((STEPS, 2, 2)),
            dma((STEPS, 2, 2)),
            dma((STEPS, 2, 2)),
            dma((2,)),
            dma((CHUNKS, 2, 2)),
            dma((CHUNKS, 2, 2)),
        ],
        compiler_params=pltpu.CompilerParams(collective_id=0, has_side_effects=True, vmem_limit_bytes=56 << 20),
        name="exchange",
    )(voltages, taps, table)


def correlate_kernel(
    rows_hbm, near_hbm, far_hbm, crossed_hbm, out_hbm,
    rows_ref, near_ref, far_ref, crossed_ref, out_ref, load_sem, out_sem,
):
    z, xl = lax.axis_index("row"), lax.axis_index("col")

    def channels(g):
        return pl.ds(g * STEP_CHAN, STEP_CHAN)

    def loads(g):
        some = channels(g)
        pairs = [(rows_hbm.at[some], rows_ref.at[some]), (near_hbm.at[some], near_ref.at[some])]
        pairs += [(far_hbm.at[some], far_ref.at[some]), (crossed_hbm.at[:, some], crossed_ref.at[:, some])]
        return [pltpu.make_async_copy(a, b, load_sem.at[g, i]) for i, (a, b) in enumerate(pairs)]

    def store(g):
        return pltpu.make_async_copy(out_ref.at[channels(g)], out_hbm.at[channels(g)], out_sem.at[g])

    groups = LOCAL_CHAN // STEP_CHAN

    @pl.loop(0, groups)
    def _(g):
        for copy in loads(g):
            copy.start()

    @pl.loop(0, groups)
    def _(g):
        for copy in loads(g):
            copy.wait()
        down_share = lax.rem(g // (FOLD_CHAN // STEP_CHAN), 2)
        near_plane = lax.rem(z + 3 + 2 * down_share, 4)
        far_plane = lax.rem(z + 2, 4)
        crossed_plane = lax.rem(z + 1 + 2 * down_share, 4)
        for index in range(STEP_CHAN):
            c = g * STEP_CHAN + index
            start = pl.multiple_of(xl * 64, 64)
            parts = []
            for part in range(2):
                pieces = [rows_ref[c, part, pl.ds(start, 64)], near_ref[c, part], far_ref[c, part]]
                parts.append(jnp.concatenate(pieces, axis=0))
            value = lax.dot_general(
                jnp.concatenate(parts, axis=1), stacked(rows_ref[c, 0], rows_ref[c, 1]), (((1,), (1,)), ((), ())),
                preferred_element_type=F32,
            )
            value = value * (1.0 / SPEC)
            for index, plane in enumerate((z, near_plane, far_plane)):
                out_ref[c, 0, plane] = value[index * 64 : index * 64 + 64, :128]
                out_ref[c, 1, plane] = value[index * 64 : index * 64 + 64, 128:]
            sides = [crossed_ref[side, c].astype(F32) for side in range(2)]
            out_ref[c, 0, crossed_plane] = jnp.concatenate([side[:, :64] for side in sides], axis=1)
            out_ref[c, 1, crossed_plane] = jnp.concatenate([side[:, 64:] for side in sides], axis=1)
        store(g).start()

    @pl.loop(0, groups)
    def _(g):
        store(g).wait()


def correlate(rows, near, far, crossed):
    any_space = pl.BlockSpec(memory_space=pl.ANY)
    groups = LOCAL_CHAN // STEP_CHAN
    return pl.pallas_call(
        correlate_kernel,
        in_specs=[any_space] * 4,
        out_specs=any_space,
        out_shape=jax.ShapeDtypeStruct((LOCAL_CHAN, 2, 4, 64, 128), F32),
        scratch_shapes=[
            pltpu.VMEM(rows.shape, BF16),
            pltpu.VMEM(near.shape, BF16),
            pltpu.VMEM(far.shape, BF16),
            pltpu.VMEM(crossed.shape, BF16),
            pltpu.VMEM((LOCAL_CHAN, 2, 4, 64, 128), F32),
            pltpu.SemaphoreType.DMA((groups, 4)),
            pltpu.SemaphoreType.DMA((groups,)),
        ],
        compiler_params=pltpu.CompilerParams(vmem_limit_bytes=58 << 20),
        name="correlate",
    )(rows, near, far, crossed)


def shards(table, voltages, tap_table):
    rows, near, far, crossed = exchange(jnp.transpose(voltages, (1, 0, 2)), tap_table, table)
    rows = rows.reshape(LOCAL_CHAN, 2, 128, SPEC)
    near = near.reshape(LOCAL_CHAN, 2, 64, SPEC)
    far = far.reshape(LOCAL_CHAN, 2, 64, SPEC)
    crossed = crossed.reshape(2, LOCAL_CHAN, 64, 128)
    return correlate(rows, near, far, crossed)


def solution(mesh):
    table = dft_tables()

    def run(voltages, tap_table):
        return jax.shard_map(
            shards,
            mesh=mesh,
            in_specs=(P(), P(("row", "col", "freq"), None, None), P()),
            out_specs=P("freq", None, None, "col", "row"),
            check_vma=False,
        )(jnp.asarray(table), voltages, tap_table)

    return run
```

```python
import math

import jax
import jax.numpy as jnp
import ml_dtypes
import numpy as np
from jax import lax
from jax.experimental import pallas as pl
from jax.experimental.pallas import tpu as pltpu
from jax.sharding import PartitionSpec as P

NFFT = 2048
HALF = NFFT // 2
TAPS = 4
SPEC = 256
CHAN = 1024
GROUPS = 16
LOCAL_CHAN = CHAN // GROUPS
CHUNKS = 4
CHUNK_CHAN = LOCAL_CHAN // CHUNKS
FOLD_CHAN = CHUNK_CHAN // 2
TARGETS = 8
ROWS = 2 * TARGETS * FOLD_CHAN
HALF_SPEC = SPEC // 2
STEPS = 2 * CHUNKS
STEP_CHAN = 4
SLOTS = 6
PAIR_LAG = 2
PASS_LAG = 3
BACK_LAG = 4
F32 = jnp.float32
BF16 = jnp.bfloat16
MESH = pl.DeviceIdType.MESH


def dft_tables():
    core, chunk, parity, part, target, index = np.meshgrid(
        np.arange(2), np.arange(CHUNKS), np.arange(2), np.arange(2), np.arange(TARGETS), np.arange(FOLD_CHAN),
        indexing="ij",
    )
    channel = (target * 2 + core) * LOCAL_CHAN + chunk * CHUNK_CHAN + 2 * index + parity
    phase = (channel[..., None] * np.arange(HALF)) % NFFT
    angle = phase * (2.0 * np.pi / NFFT)
    cosine = np.where(phase % (NFFT // 2) == NFFT // 4, 0.0, np.cos(angle))
    sine = np.where(phase % (NFFT // 2) == 0, 0.0, np.sin(angle))
    values = np.where(part[..., None] == 0, cosine, -sine) / (64.0 * math.sqrt(NFFT) * 4096.0)
    high = values.astype(ml_dtypes.bfloat16)
    low = (values - high.astype(np.float64)).astype(ml_dtypes.bfloat16)
    shape = (2, CHUNKS, 2, ROWS, HALF)
    return np.concatenate([high.reshape(shape), low.reshape(shape)], axis=3)


def filter_half(half, source, first, taps_ref, frames, mixed, folded):
    count = 4 * (HALF_SPEC + TAPS - 1)

    @pl.loop(0, HALF // 128)
    def _(step):
        low = pl.multiple_of(step * 128, 128)
        columns = (low, pl.multiple_of(low + HALF, 128))
        weights = []
        for side in range(2):
            block = source[pl.ds(half * HALF_SPEC, HALF_SPEC + TAPS - 1), :, pl.ds(columns[side], 128)]
            frames[side, 0:count, :] = block.astype(F32).reshape(count, 128)
            weights.append([taps_ref[pl.ds(tap, 1), pl.ds(columns[side], 128)].astype(F32) for tap in range(TAPS)])
        for start in range(0, 4 * HALF_SPEC, 64):
            sides = []
            for side in range(2):
                even = frames[side, start : start + 72, :]
                odd = frames[side, start + 4 : start + 76, :]
                w = weights[side]
                sides.append(w[0] * even[:64] + w[1] * odd[:64] + w[2] * even[8:] + w[3] * odd[8:])
            mixed[0, start : start + 64, :] = sides[0] + sides[1]
            mixed[1, start : start + 64, :] = sides[0] - sides[1]
        for row in range(4):
            slot = first + row
            place = (slot % 2) * HALF_SPEC
            for parity in range(2):
                value = mixed[parity, pl.ds(row, HALF_SPEC, stride=4), :]
                top = value.astype(BF16)
                rest = (value - top.astype(F32)).astype(BF16)
                folded[parity, 0, half, slot // 2, place : place + HALF_SPEC, pl.ds(low, 128)] = top
                folded[parity, 1, half, slot // 2, place : place + HALF_SPEC, pl.ds(low, 128)] = rest


def transform_chunk(half, quarter, core, table_ref, folded, turned, write):
    contract = (((1,), (1,)), ((), ()))

    @pl.loop(0, 4)
    def _(duo):
        for parity in range(2):
            top = folded[parity, 0, half, duo]
            both = lax.dot_general(table_ref[quarter, parity], top, contract, preferred_element_type=F32)
            rest = lax.dot_general(
                table_ref[quarter, parity, :ROWS], folded[parity, 1, half, duo], contract, preferred_element_type=F32
            )
            value = both[:ROWS] + both[ROWS:] + rest
            for sub in range(2):
                row = lax.rem(2 * duo + sub + 4 * core, 8)
                for part in range(2):
                    turned[pl.ds(parity * 16 + part * 8 + row, ROWS // 2, stride=32), :] = value[
                        part * (ROWS // 2) : (part + 1) * (ROWS // 2), sub * 128 : sub * 128 + 128
                    ]

    block = CHUNK_CHAN * 16

    @pl.loop(0, TARGETS)
    def _(target):
        rows = turned[pl.ds(pl.multiple_of(target * block, block), block), :]
        write(target, rows.reshape(2 * CHUNK_CHAN, 8, 128).astype(BF16))


def stacked(real, imag):
    return jnp.concatenate([jnp.concatenate([real, imag], axis=1), jnp.concatenate([imag, -real], axis=1)], axis=0)


def exchange_kernel(
    own_ref, taps_ref, table_hbm, rows, near, far, crossed,
    own, other, table, frames, mixed, folded, turned, made, products,
    load_sem, table_sem, core_send, core_recv,
    local_sem, first_send, first_recv, pair_send, pair_recv, ring_send, ring_recv, pass_send, pass_recv,
    back_send, back_recv,
):
    freq, z, xl = lax.axis_index("freq"), lax.axis_index("row"), lax.axis_index("col")
    core = lax.rem(freq, 2)
    xh = lax.rem(freq // 2, 2)
    y = freq // 4
    up, down = lax.rem(z + 1, 4), lax.rem(z + 3, 4)
    pieces = (pl.ds(0, HALF_SPEC + TAPS - 1), pl.ds(HALF_SPEC + TAPS - 1, HALF_SPEC))

    def load(part):
        return pltpu.make_async_copy(own_ref.at[pieces[part]], own.at[pieces[part]], load_sem.at[part])

    def load_table(quarter):
        return pltpu.make_async_copy(table_hbm.at[core, quarter], table.at[quarter], table_sem.at[quarter])

    load(0).start()
    for quarter in range(CHUNKS):
        load_table(quarter).start()
    load(1).start()

    def device(to_y, to_xh, to_z, to_xl, to_core=core):
        return {"freq": (to_y * 2 + to_xh) * 2 + to_core, "row": to_z, "col": to_xl}

    sibling = device(y, xh, z, xl, 1 - core)
    partner = device(y, xh, z, 1 - xl)
    above, below = device(y, xh, up, xl), device(y, xh, down, xl)

    barrier = pltpu.get_barrier_semaphore()
    others = [sibling]
    others += [device(lax.rem(y + step, 4), xh, z, xl) for step in range(1, 4)]
    others += [device(lax.rem(y + step, 4), 1 - xh, z, 1 - xl) for step in range(4)]
    others += [partner, above, below, device(y, xh, up, 1 - xl), device(y, xh, down, 1 - xl)]
    for one in others:
        pl.semaphore_signal(barrier, inc=1, device_id=one, device_id_type=MESH)
    pl.semaphore_wait(barrier, len(others))

    def remote(source, target, send, recv, where):
        return pltpu.make_async_remote_copy(
            src_ref=source, dst_ref=target, send_sem=send, recv_sem=recv, device_id=where, device_id_type=MESH
        )

    def swap(part):
        return remote(
            own_ref.at[pieces[part]], other.at[pieces[part]], core_send.at[part], core_recv.at[part], sibling
        )

    for part in range(2):
        swap(part).start()

    def spot(t):
        return lax.rem(t, CHUNKS), pl.ds(pl.multiple_of((t // CHUNKS) * HALF_SPEC, HALF_SPEC), HALF_SPEC)

    def home(t, side, from_y, from_xh):
        k, lanes = spot(t)
        return rows.at[k, :, side, from_y, from_xh, :, lanes]

    def first(t, step, flip):
        to_y, to_xh, to_xl = lax.rem(y + step, 4), (1 - xh if flip else xh), (1 - xl if flip else xl)
        index = flip * 4 + step
        return remote(
            made.at[t, to_y * 2 + to_xh], home(t, xl, y, xh),
            first_send.at[t, index], first_recv.at[t, index], device(to_y, to_xh, z, to_xl),
        )

    def first_arrival(t, step, flip):
        from_y, from_xh, from_xl = lax.rem(y + 4 - step, 4), (1 - xh if flip else xh), (1 - xl if flip else xl)
        index = flip * 4 + step
        place = home(t, from_xl, from_y, from_xh)
        return remote(
            place, place, first_send.at[t, index], first_recv.at[t, index], device(from_y, from_xh, z, from_xl)
        )

    def local(t):
        return pltpu.make_async_copy(made.at[t, y * 2 + xh], home(t, xl, y, xh), local_sem.at[t])

    def pair(t, part, mine=True):
        k, lanes = spot(t)
        side = xl if (part == 0) == mine else 1 - xl
        place = rows.at[k, :, side, :, xh if part == 0 else 1 - xh, :, lanes]
        return remote(place, place, pair_send.at[t, part], pair_recv.at[t, part], partner)

    def ring(t, part, way):
        k, lanes = spot(t)
        column = xh if part == 0 else 1 - xh
        share = pl.ds(way * CHUNK_CHAN, CHUNK_CHAN)
        return remote(
            rows.at[k, share, xl, :, column, :, lanes], near.at[k, share, :, column, :, lanes],
            ring_send.at[t, part, way], ring_recv.at[t, part, way], above if way == 0 else below,
        )

    def onward(t, part, way):
        k, lanes = spot(t)
        column = xh if part == 0 else 1 - xh
        share = pl.ds(way * CHUNK_CHAN, CHUNK_CHAN)
        return remote(
            near.at[k, share, :, column, :, lanes], far.at[k, share, :, column, :, lanes],
            pass_send.at[t, part, way], pass_recv.at[t, part, way], above if way == 0 else below,
        )

    def back(k, way, side):
        share = pl.ds(way * FOLD_CHAN, FOLD_CHAN)
        return remote(
            products.at[k, side, share], crossed.at[xl, k, share],
            back_send.at[k, way, side], back_recv.at[k, way, xl],
            device(y, xh, down if way == 0 else up, side),
        )

    def back_arrival(k, way, side):
        share = pl.ds(way * FOLD_CHAN, FOLD_CHAN)
        place = crossed.at[side, k, share]
        return remote(
            place, place, back_send.at[k, way, side], back_recv.at[k, way, side],
            device(y, xh, up if way == 0 else down, side),
        )

    def multiply(k):
        @pl.loop(0, CHUNK_CHAN)
        def _(c):
            left = [rows[k, 2 * c + part].reshape(128, SPEC) for part in range(2)]
            right = [near[k, 2 * c + part].reshape(64, SPEC) for part in range(2)]
            value = lax.dot_general(
                jnp.concatenate(left, axis=1), stacked(right[0], right[1]), (((1,), (1,)), ((), ())),
                preferred_element_type=F32,
            )
            value = (value * (1.0 / SPEC)).astype(BF16)
            products[k, 0, c] = value[:64]
            products[k, 1, c] = value[64:]

        for way in range(2):
            for side in range(2):
                back(k, way, side).start()

    def fold(half):
        load(half).wait()
        filter_half(half, own, 0, taps_ref, frames, mixed, folded)
        swap(half).wait_recv()
        filter_half(half, other, 4, taps_ref, frames, mixed, folded)

    fold(0)
    for quarter in range(CHUNKS):
        load_table(quarter).wait()

    @pl.loop(0, STEPS + BACK_LAG)
    def _(turn):
        @pl.when(turn == CHUNKS)
        def _():
            fold(1)

        @pl.when(turn < STEPS)
        def _():
            def write(target, value):
                made[turn, target] = value

            transform_chunk(turn // CHUNKS, lax.rem(turn, CHUNKS), core, table, folded, turned, write)
            local(turn).start()
            for step in range(1, 4):
                first(turn, step, 0).start()
            for step in range(4):
                first(turn, step, 1).start()

        @pl.when((turn >= 1) & (turn <= STEPS))
        def _():
            t = turn - 1
            local(t).wait()
            for step in range(1, 4):
                first_arrival(t, step, 0).wait_recv()
            for way in range(2):
                ring(t, 0, way).start()
            for step in range(4):
                first_arrival(t, step, 1).wait_recv()
            pair(t, 1).start()
            pair(t, 0).start()

        @pl.when((turn >= PAIR_LAG) & (turn < STEPS + PAIR_LAG))
        def _():
            t = turn - PAIR_LAG
            pair(t, 1, False).wait_recv()
            for way in range(2):
                ring(t, 1, way).start()

        @pl.when((turn >= PASS_LAG) & (turn < STEPS + PASS_LAG))
        def _():
            t = turn - PASS_LAG
            for part in range(2):
                for way in range(2):
                    ring(t, part, way).wait_recv()
                    onward(t, part, way).start()
            pair(t, 0, False).wait_recv()

        @pl.when(turn >= CHUNKS + BACK_LAG)
        def _():
            multiply(turn - CHUNKS - BACK_LAG)

    for part in range(2):
        swap(part).wait_send()

    @pl.loop(0, CHUNKS)
    def _(k):
        for way in range(2):
            for side in range(2):
                back_arrival(k, way, side).wait_recv()
                back(k, way, side).wait_send()

    @pl.loop(0, STEPS)
    def _(t):
        for step in range(1, 4):
            first(t, step, 0).wait_send()
        for step in range(4):
            first(t, step, 1).wait_send()
        for part in range(2):
            pair(t, part).wait_send()
            for way in range(2):
                ring(t, part, way).wait_send()
                onward(t, part, way).wait_recv()
                onward(t, part, way).wait_send()


def exchange(voltages, taps, table):
    any_space = pl.BlockSpec(memory_space=pl.ANY)
    dma = pltpu.SemaphoreType.DMA
    return pl.pallas_call(
        exchange_kernel,
        in_specs=[any_space, pl.BlockSpec(memory_space=pltpu.VMEM), any_space],
        out_specs=[pl.BlockSpec(memory_space=pltpu.VMEM)] * 4,
        out_shape=[
            pltpu.VMEM((CHUNKS, 2 * CHUNK_CHAN, 2, 4, 2, 8, SPEC), BF16),
            pltpu.VMEM((CHUNKS, 2 * CHUNK_CHAN, 4, 2, 8, SPEC), BF16),
            pltpu.VMEM((CHUNKS, 2 * CHUNK_CHAN, 4, 2, 8, SPEC), BF16),
            pltpu.VMEM((2, CHUNKS, CHUNK_CHAN, 64, 128), BF16),
        ],
        scratch_shapes=[
            pltpu.VMEM(voltages.shape, BF16),
            pltpu.VMEM(voltages.shape, BF16),
            pltpu.VMEM(table.shape[1:], BF16),
            pltpu.VMEM((2, 4 * 132, 128), F32),
            pltpu.VMEM((2, 4 * HALF_SPEC, 128), F32),
            pltpu.VMEM((2, 2, 2, 4, 2 * HALF_SPEC, HALF), BF16),
            pltpu.VMEM((TARGETS * CHUNK_CHAN * 16, 128), F32),
            pltpu.VMEM((STEPS, TARGETS, 2 * CHUNK_CHAN, 8, HALF_SPEC), BF16),
            pltpu.VMEM((CHUNKS, 2, CHUNK_CHAN, 64, 128), BF16),
            dma((2,)),
            dma((CHUNKS,)),
            dma((2,)),
            dma((2,)),
            dma((STEPS,)),
            dma((STEPS, 8)),
            dma((STEPS, 8)),
            dma((STEPS, 2)),
            dma((STEPS, 2)),
            dma((STEPS, 2, 2)),
            dma((STEPS, 2, 2)),
            dma((STEPS, 2, 2)),
            dma((STEPS, 2, 2)),
            dma((CHUNKS, 2, 2)),
            dma((CHUNKS, 2, 2)),
        ],
        compiler_params=pltpu.CompilerParams(collective_id=0, has_side_effects=True, vmem_limit_bytes=40 << 20),
        name="exchange",
    )(voltages, taps, table)


def correlate_kernel(rows, near, far, crossed, out_hbm, out_ref, out_sem):
    z, xl = lax.axis_index("row"), lax.axis_index("col")
    groups = LOCAL_CHAN // STEP_CHAN

    def store(g):
        slot = lax.rem(g, SLOTS)
        return pltpu.make_async_copy(
            out_ref.at[slot], out_hbm.at[pl.ds(g * STEP_CHAN, STEP_CHAN)], out_sem.at[slot]
        )

    @pl.loop(0, groups)
    def _(g):
        @pl.when(g >= SLOTS)
        def _():
            store(g - SLOTS).wait()

        slot = lax.rem(g, SLOTS)
        k = g * STEP_CHAN // CHUNK_CHAN
        down_share = lax.rem(g // (FOLD_CHAN // STEP_CHAN), 2)
        near_plane = lax.rem(z + 3 + 2 * down_share, 4)
        far_plane = lax.rem(z + 2, 4)
        crossed_plane = lax.rem(z + 1 + 2 * down_share, 4)
        for c in range(STEP_CHAN):
            place = lax.rem(g * STEP_CHAN, CHUNK_CHAN) + c
            parts = []
            for part in range(2):
                pieces = [rows[k, 2 * place + part, xl], near[k, 2 * place + part], far[k, 2 * place + part]]
                parts.append(jnp.concatenate([piece.reshape(64, SPEC) for piece in pieces], axis=0))
            row_side = [rows[k, 2 * place + part].reshape(128, SPEC) for part in range(2)]
            both = lax.dot_general(
                jnp.concatenate(parts, axis=0), jnp.concatenate(row_side, axis=0), (((1,), (1,)), ((), ())),
                preferred_element_type=F32,
            )
            value = jnp.concatenate(
                [both[:192, :128] + both[192:, 128:], both[:192, 128:] - both[192:, :128]], axis=1
            ) * (1.0 / SPEC)
            for index, plane in enumerate((z, near_plane, far_plane)):
                out_ref[slot, c, 0, plane] = value[index * 64 : index * 64 + 64, :128]
                out_ref[slot, c, 1, plane] = value[index * 64 : index * 64 + 64, 128:]
            sides = [crossed[side, k, place].astype(F32) for side in range(2)]
            out_ref[slot, c, 0, crossed_plane] = jnp.concatenate([side[:, :64] for side in sides], axis=1)
            out_ref[slot, c, 1, crossed_plane] = jnp.concatenate([side[:, 64:] for side in sides], axis=1)
        store(g).start()

    @pl.loop(groups - SLOTS, groups)
    def _(g):
        store(g).wait()


def correlate(rows, near, far, crossed):
    return pl.pallas_call(
        correlate_kernel,
        in_specs=[pl.BlockSpec(memory_space=pltpu.VMEM)] * 4,
        out_specs=pl.BlockSpec(memory_space=pl.ANY),
        out_shape=jax.ShapeDtypeStruct((LOCAL_CHAN, 2, 4, 64, 128), F32),
        scratch_shapes=[
            pltpu.VMEM((SLOTS, STEP_CHAN, 2, 4, 64, 128), F32),
            pltpu.SemaphoreType.DMA((SLOTS,)),
        ],
        compiler_params=pltpu.CompilerParams(vmem_limit_bytes=20 << 20),
        name="correlate",
    )(rows, near, far, crossed)


def shards(table, voltages, tap_table):
    rows, near, far, crossed = exchange(jnp.transpose(voltages, (1, 0, 2)), tap_table, table)
    return correlate(rows, near, far, crossed)


def solution(mesh):
    table = dft_tables()

    def run(voltages, tap_table):
        return jax.shard_map(
            shards,
            mesh=mesh,
            in_specs=(P(), P(("row", "col", "freq"), None, None), P()),
            out_specs=P("freq", None, None, "col", "row"),
            check_vma=False,
        )(jnp.asarray(table), voltages, tap_table)

    return run
```

```python
import math

import jax
import jax.numpy as jnp
import ml_dtypes
import numpy as np
from jax import lax
from jax.experimental import pallas as pl
from jax.experimental.pallas import tpu as pltpu
from jax.sharding import PartitionSpec as P

NFFT = 2048
HALF = NFFT // 2
TAPS = 4
SPEC = 256
CHAN = 1024
GROUPS = 16
LOCAL_CHAN = CHAN // GROUPS
CHUNKS = 4
CHUNK_CHAN = LOCAL_CHAN // CHUNKS
FOLD_CHAN = CHUNK_CHAN // 2
TARGETS = 8
ROWS = 2 * TARGETS * FOLD_CHAN
HALF_SPEC = SPEC // 2
STEPS = 2 * CHUNKS
STEP_CHAN = 4
SLOTS = 6
PAIR_LAG = 2
PASS_LAG = 3
BACK_LAG = 4
F32 = jnp.float32
BF16 = jnp.bfloat16
MESH = pl.DeviceIdType.MESH


def dft_tables():
    core, chunk, parity, part, target, index = np.meshgrid(
        np.arange(2), np.arange(CHUNKS), np.arange(2), np.arange(2), np.arange(TARGETS), np.arange(FOLD_CHAN),
        indexing="ij",
    )
    channel = (target * 2 + core) * LOCAL_CHAN + chunk * CHUNK_CHAN + 2 * index + parity
    phase = (channel[..., None] * np.arange(HALF)) % NFFT
    angle = phase * (2.0 * np.pi / NFFT)
    cosine = np.where(phase % (NFFT // 2) == NFFT // 4, 0.0, np.cos(angle))
    sine = np.where(phase % (NFFT // 2) == 0, 0.0, np.sin(angle))
    values = np.where(part[..., None] == 0, cosine, -sine) / (64.0 * math.sqrt(NFFT) * 4096.0)
    high = values.astype(ml_dtypes.bfloat16)
    low = (values - high.astype(np.float64)).astype(ml_dtypes.bfloat16)
    shape = (2, CHUNKS, 2, ROWS, HALF)
    return np.concatenate([high.reshape(shape), low.reshape(shape)], axis=3)


def filter_half(half, source, first, taps_ref, frames, mixed, folded):
    count = 4 * (HALF_SPEC + TAPS - 1)

    @pl.loop(0, HALF // 128)
    def _(step):
        low = pl.multiple_of(step * 128, 128)
        columns = (low, pl.multiple_of(low + HALF, 128))
        weights = []
        for side in range(2):
            block = source[pl.ds(half * HALF_SPEC, HALF_SPEC + TAPS - 1), :, pl.ds(columns[side], 128)]
            frames[side, 0:count, :] = block.astype(F32).reshape(count, 128)
            weights.append([taps_ref[pl.ds(tap, 1), pl.ds(columns[side], 128)].astype(F32) for tap in range(TAPS)])
        for start in range(0, 4 * HALF_SPEC, 64):
            sides = []
            for side in range(2):
                even = frames[side, start : start + 72, :]
                odd = frames[side, start + 4 : start + 76, :]
                w = weights[side]
                sides.append(w[0] * even[:64] + w[1] * odd[:64] + w[2] * even[8:] + w[3] * odd[8:])
            mixed[0, start : start + 64, :] = sides[0] + sides[1]
            mixed[1, start : start + 64, :] = sides[0] - sides[1]
        for row in range(4):
            slot = first + row
            place = (slot % 2) * HALF_SPEC
            for parity in range(2):
                value = mixed[parity, pl.ds(row, HALF_SPEC, stride=4), :]
                top = value.astype(BF16)
                rest = (value - top.astype(F32)).astype(BF16)
                folded[parity, 0, half, slot // 2, place : place + HALF_SPEC, pl.ds(low, 128)] = top
                folded[parity, 1, half, slot // 2, place : place + HALF_SPEC, pl.ds(low, 128)] = rest


def transform_rows(half, quarter, core, table_ref, folded, turned, first_duo, last_duo):
    contract = (((1,), (1,)), ((), ()))

    @pl.loop(first_duo, last_duo)
    def _(duo):
        for parity in range(2):
            top = folded[parity, 0, half, duo]
            both = lax.dot_general(table_ref[quarter, parity], top, contract, preferred_element_type=F32)
            rest = lax.dot_general(
                table_ref[quarter, parity, :ROWS], folded[parity, 1, half, duo], contract, preferred_element_type=F32
            )
            value = both[:ROWS] + both[ROWS:] + rest
            for sub in range(2):
                row = lax.rem(2 * duo + sub + 4 * core, 8)
                for part in range(2):
                    turned[pl.ds(parity * 16 + part * 8 + row, ROWS // 2, stride=32), :] = value[
                        part * (ROWS // 2) : (part + 1) * (ROWS // 2), sub * 128 : sub * 128 + 128
                    ]


def round_rows(turned, write):
    block = CHUNK_CHAN * 16

    @pl.loop(0, TARGETS)
    def _(target):
        rows = turned[pl.ds(pl.multiple_of(target * block, block), block), :]
        write(target, rows.reshape(2 * CHUNK_CHAN, 8, 128).astype(BF16))


def stacked(real, imag):
    return jnp.concatenate([jnp.concatenate([real, imag], axis=1), jnp.concatenate([imag, -real], axis=1)], axis=0)


def exchange_kernel(
    own_ref, taps_ref, table_hbm, rows, near, far, crossed,
    own, other, table, frames, mixed, folded, turned, made, products,
    load_sem, table_sem, core_send, core_recv,
    local_sem, first_send, first_recv, pair_send, pair_recv, ring_send, ring_recv, pass_send, pass_recv,
    back_send, back_recv,
):
    freq, z, xl = lax.axis_index("freq"), lax.axis_index("row"), lax.axis_index("col")
    core = lax.rem(freq, 2)
    xh = lax.rem(freq // 2, 2)
    y = freq // 4
    up, down = lax.rem(z + 1, 4), lax.rem(z + 3, 4)
    pieces = (pl.ds(0, HALF_SPEC + TAPS - 1), pl.ds(HALF_SPEC + TAPS - 1, HALF_SPEC))

    def load(part):
        return pltpu.make_async_copy(own_ref.at[pieces[part]], own.at[pieces[part]], load_sem.at[part])

    def load_table(quarter):
        return pltpu.make_async_copy(table_hbm.at[core, quarter], table.at[quarter], table_sem.at[quarter])

    load(0).start()
    for quarter in range(CHUNKS):
        load_table(quarter).start()
    load(1).start()

    def device(to_y, to_xh, to_z, to_xl, to_core=core):
        return {"freq": (to_y * 2 + to_xh) * 2 + to_core, "row": to_z, "col": to_xl}

    sibling = device(y, xh, z, xl, 1 - core)
    partner = device(y, xh, z, 1 - xl)
    above, below = device(y, xh, up, xl), device(y, xh, down, xl)

    barrier = pltpu.get_barrier_semaphore()
    others = [sibling]
    others += [device(lax.rem(y + step, 4), xh, z, xl) for step in range(1, 4)]
    others += [device(lax.rem(y + step, 4), 1 - xh, z, 1 - xl) for step in range(4)]
    others += [partner, above, below, device(y, xh, up, 1 - xl), device(y, xh, down, 1 - xl)]
    for one in others:
        pl.semaphore_signal(barrier, inc=1, device_id=one, device_id_type=MESH)
    pl.semaphore_wait(barrier, len(others))

    def remote(source, target, send, recv, where):
        return pltpu.make_async_remote_copy(
            src_ref=source, dst_ref=target, send_sem=send, recv_sem=recv, device_id=where, device_id_type=MESH
        )

    def swap(part):
        return remote(
            own_ref.at[pieces[part]], other.at[pieces[part]], core_send.at[part], core_recv.at[part], sibling
        )

    for part in range(2):
        swap(part).start()

    def spot(t):
        return lax.rem(t, CHUNKS), pl.ds(pl.multiple_of((t // CHUNKS) * HALF_SPEC, HALF_SPEC), HALF_SPEC)

    def home(t, side, from_y, from_xh):
        k, lanes = spot(t)
        return rows.at[k, :, side, from_y, from_xh, :, lanes]

    def first(t, step, flip):
        to_y, to_xh, to_xl = lax.rem(y + step, 4), (1 - xh if flip else xh), (1 - xl if flip else xl)
        index = flip * 4 + step
        return remote(
            made.at[t, to_y * 2 + to_xh], home(t, xl, y, xh),
            first_send.at[t, index], first_recv.at[t, index], device(to_y, to_xh, z, to_xl),
        )

    def first_arrival(t, step, flip):
        from_y, from_xh, from_xl = lax.rem(y + 4 - step, 4), (1 - xh if flip else xh), (1 - xl if flip else xl)
        index = flip * 4 + step
        place = home(t, from_xl, from_y, from_xh)
        return remote(
            place, place, first_send.at[t, index], first_recv.at[t, index], device(from_y, from_xh, z, from_xl)
        )

    def local(t):
        return pltpu.make_async_copy(made.at[t, y * 2 + xh], home(t, xl, y, xh), local_sem.at[t])

    def pair(t, part, mine=True):
        k, lanes = spot(t)
        side = xl if (part == 0) == mine else 1 - xl
        place = rows.at[k, :, side, :, xh if part == 0 else 1 - xh, :, lanes]
        return remote(place, place, pair_send.at[t, part], pair_recv.at[t, part], partner)

    def ring(t, part, way):
        k, lanes = spot(t)
        column = xh if part == 0 else 1 - xh
        share = pl.ds(way * CHUNK_CHAN, CHUNK_CHAN)
        return remote(
            rows.at[k, share, xl, :, column, :, lanes], near.at[k, share, :, column, :, lanes],
            ring_send.at[t, part, way], ring_recv.at[t, part, way], above if way == 0 else below,
        )

    def onward(t, part, way):
        k, lanes = spot(t)
        column = xh if part == 0 else 1 - xh
        share = pl.ds(way * CHUNK_CHAN, CHUNK_CHAN)
        return remote(
            near.at[k, share, :, column, :, lanes], far.at[k, share, :, column, :, lanes],
            pass_send.at[t, part, way], pass_recv.at[t, part, way], above if way == 0 else below,
        )

    def back(k, way, side):
        share = pl.ds(way * FOLD_CHAN, FOLD_CHAN)
        return remote(
            products.at[k, side, share], crossed.at[xl, k, share],
            back_send.at[k, way, side], back_recv.at[k, way, xl],
            device(y, xh, down if way == 0 else up, side),
        )

    def back_arrival(k, way, side):
        share = pl.ds(way * FOLD_CHAN, FOLD_CHAN)
        place = crossed.at[side, k, share]
        return remote(
            place, place, back_send.at[k, way, side], back_recv.at[k, way, side],
            device(y, xh, up if way == 0 else down, side),
        )

    def multiply(k):
        for way in range(2):

            @pl.loop(way * FOLD_CHAN, (way + 1) * FOLD_CHAN)
            def _(c):
                left = [rows[k, 2 * c + part].reshape(128, SPEC) for part in range(2)]
                right = [near[k, 2 * c + part].reshape(64, SPEC) for part in range(2)]
                value = lax.dot_general(
                    jnp.concatenate(left, axis=1), stacked(right[0], right[1]), (((1,), (1,)), ((), ())),
                    preferred_element_type=F32,
                )
                value = (value * (1.0 / SPEC)).astype(BF16)
                products[k, 0, c] = value[:64]
                products[k, 1, c] = value[64:]

            for side in range(2):
                back(k, way, side).start()

    def fold_own(half):
        load(half).wait()
        filter_half(half, own, 0, taps_ref, frames, mixed, folded)

    def fold_other(half):
        swap(half).wait_recv()
        filter_half(half, other, 4, taps_ref, frames, mixed, folded)

    fold_own(0)
    load_table(0).wait()
    transform_rows(0, 0, core, table, folded, turned, 0, 2)
    fold_other(0)
    for quarter in range(1, CHUNKS):
        load_table(quarter).wait()

    @pl.loop(0, STEPS + BACK_LAG)
    def _(turn):
        @pl.when(turn == CHUNKS)
        def _():
            fold_own(1)
            fold_other(1)

        @pl.when(turn < STEPS)
        def _():
            def write(target, value):
                made[turn, target] = value

            first_duo = 2 - 2 * lax.min(turn, 1)
            transform_rows(turn // CHUNKS, lax.rem(turn, CHUNKS), core, table, folded, turned, first_duo, 4)
            round_rows(turned, write)
            local(turn).start()
            for step in range(1, 4):
                first(turn, step, 0).start()
            for step in range(4):
                first(turn, step, 1).start()

        @pl.when((turn >= 1) & (turn <= STEPS))
        def _():
            t = turn - 1
            local(t).wait()
            for step in range(1, 4):
                first_arrival(t, step, 0).wait_recv()
            for way in range(2):
                ring(t, 0, way).start()
            for step in range(4):
                first_arrival(t, step, 1).wait_recv()
            pair(t, 1).start()
            pair(t, 0).start()

        @pl.when((turn >= PAIR_LAG) & (turn < STEPS + PAIR_LAG))
        def _():
            t = turn - PAIR_LAG
            pair(t, 1, False).wait_recv()
            for way in range(2):
                ring(t, 1, way).start()

        @pl.when((turn >= PASS_LAG) & (turn < STEPS + PASS_LAG))
        def _():
            t = turn - PASS_LAG
            for part in range(2):
                for way in range(2):
                    ring(t, part, way).wait_recv()
                    onward(t, part, way).start()
            pair(t, 0, False).wait_recv()

        @pl.when(turn >= CHUNKS + BACK_LAG)
        def _():
            multiply(turn - CHUNKS - BACK_LAG)

    for part in range(2):
        swap(part).wait_send()

    @pl.loop(0, CHUNKS)
    def _(k):
        for way in range(2):
            for side in range(2):
                back_arrival(k, way, side).wait_recv()
                back(k, way, side).wait_send()

    @pl.loop(0, STEPS)
    def _(t):
        for step in range(1, 4):
            first(t, step, 0).wait_send()
        for step in range(4):
            first(t, step, 1).wait_send()
        for part in range(2):
            pair(t, part).wait_send()
            for way in range(2):
                ring(t, part, way).wait_send()
                onward(t, part, way).wait_recv()
                onward(t, part, way).wait_send()


def exchange(voltages, taps, table):
    any_space = pl.BlockSpec(memory_space=pl.ANY)
    dma = pltpu.SemaphoreType.DMA
    return pl.pallas_call(
        exchange_kernel,
        in_specs=[any_space, pl.BlockSpec(memory_space=pltpu.VMEM), any_space],
        out_specs=[pl.BlockSpec(memory_space=pltpu.VMEM)] * 4,
        out_shape=[
            pltpu.VMEM((CHUNKS, 2 * CHUNK_CHAN, 2, 4, 2, 8, SPEC), BF16),
            pltpu.VMEM((CHUNKS, 2 * CHUNK_CHAN, 4, 2, 8, SPEC), BF16),
            pltpu.VMEM((CHUNKS, 2 * CHUNK_CHAN, 4, 2, 8, SPEC), BF16),
            pltpu.VMEM((2, CHUNKS, CHUNK_CHAN, 64, 128), BF16),
        ],
        scratch_shapes=[
            pltpu.VMEM(voltages.shape, BF16),
            pltpu.VMEM(voltages.shape, BF16),
            pltpu.VMEM(table.shape[1:], BF16),
            pltpu.VMEM((2, 4 * 132, 128), F32),
            pltpu.VMEM((2, 4 * HALF_SPEC, 128), F32),
            pltpu.VMEM((2, 2, 2, 4, 2 * HALF_SPEC, HALF), BF16),
            pltpu.VMEM((TARGETS * CHUNK_CHAN * 16, 128), F32),
            pltpu.VMEM((STEPS, TARGETS, 2 * CHUNK_CHAN, 8, HALF_SPEC), BF16),
            pltpu.VMEM((CHUNKS, 2, CHUNK_CHAN, 64, 128), BF16),
            dma((2,)),
            dma((CHUNKS,)),
            dma((2,)),
            dma((2,)),
            dma((STEPS,)),
            dma((STEPS, 8)),
            dma((STEPS, 8)),
            dma((STEPS, 2)),
            dma((STEPS, 2)),
            dma((STEPS, 2, 2)),
            dma((STEPS, 2, 2)),
            dma((STEPS, 2, 2)),
            dma((STEPS, 2, 2)),
            dma((CHUNKS, 2, 2)),
            dma((CHUNKS, 2, 2)),
        ],
        compiler_params=pltpu.CompilerParams(collective_id=0, has_side_effects=True, vmem_limit_bytes=40 << 20),
        name="exchange",
    )(voltages, taps, table)


def correlate_kernel(rows, near, far, crossed, out_hbm, out_ref, out_sem):
    z, xl = lax.axis_index("row"), lax.axis_index("col")
    groups = LOCAL_CHAN // STEP_CHAN

    def store(g):
        slot = lax.rem(g, SLOTS)
        return pltpu.make_async_copy(
            out_ref.at[slot], out_hbm.at[pl.ds(g * STEP_CHAN, STEP_CHAN)], out_sem.at[slot]
        )

    @pl.loop(0, groups)
    def _(g):
        @pl.when(g >= SLOTS)
        def _():
            store(g - SLOTS).wait()

        slot = lax.rem(g, SLOTS)
        k = g * STEP_CHAN // CHUNK_CHAN
        down_share = lax.rem(g // (FOLD_CHAN // STEP_CHAN), 2)
        near_plane = lax.rem(z + 3 + 2 * down_share, 4)
        far_plane = lax.rem(z + 2, 4)
        crossed_plane = lax.rem(z + 1 + 2 * down_share, 4)
        for c in range(STEP_CHAN):
            place = lax.rem(g * STEP_CHAN, CHUNK_CHAN) + c
            parts = []
            for part in range(2):
                pieces = [rows[k, 2 * place + part, xl], near[k, 2 * place + part], far[k, 2 * place + part]]
                parts.append(jnp.concatenate([piece.reshape(64, SPEC) for piece in pieces], axis=0))
            row_side = [rows[k, 2 * place + part].reshape(128, SPEC) for part in range(2)]
            both = lax.dot_general(
                jnp.concatenate(parts, axis=0), jnp.concatenate(row_side, axis=0), (((1,), (1,)), ((), ())),
                preferred_element_type=F32,
            )
            value = jnp.concatenate(
                [both[:192, :128] + both[192:, 128:], both[:192, 128:] - both[192:, :128]], axis=1
            ) * (1.0 / SPEC)
            for index, plane in enumerate((z, near_plane, far_plane)):
                out_ref[slot, c, 0, plane] = value[index * 64 : index * 64 + 64, :128]
                out_ref[slot, c, 1, plane] = value[index * 64 : index * 64 + 64, 128:]
            sides = [crossed[side, k, place].astype(F32) for side in range(2)]
            out_ref[slot, c, 0, crossed_plane] = jnp.concatenate([side[:, :64] for side in sides], axis=1)
            out_ref[slot, c, 1, crossed_plane] = jnp.concatenate([side[:, 64:] for side in sides], axis=1)
        store(g).start()

    @pl.loop(groups - SLOTS, groups)
    def _(g):
        store(g).wait()


def correlate(rows, near, far, crossed):
    return pl.pallas_call(
        correlate_kernel,
        in_specs=[pl.BlockSpec(memory_space=pltpu.VMEM)] * 4,
        out_specs=pl.BlockSpec(memory_space=pl.ANY),
        out_shape=jax.ShapeDtypeStruct((LOCAL_CHAN, 2, 4, 64, 128), F32),
        scratch_shapes=[
            pltpu.VMEM((SLOTS, STEP_CHAN, 2, 4, 64, 128), F32),
            pltpu.SemaphoreType.DMA((SLOTS,)),
        ],
        compiler_params=pltpu.CompilerParams(vmem_limit_bytes=20 << 20),
        name="correlate",
    )(rows, near, far, crossed)


def shards(table, voltages, tap_table):
    rows, near, far, crossed = exchange(jnp.transpose(voltages, (1, 0, 2)), tap_table, table)
    return correlate(rows, near, far, crossed)


def solution(mesh):
    table = dft_tables()

    def run(voltages, tap_table):
        return jax.shard_map(
            shards,
            mesh=mesh,
            in_specs=(P(), P(("row", "col", "freq"), None, None), P()),
            out_specs=P("freq", None, None, "col", "row"),
            check_vma=False,
        )(jnp.asarray(table), voltages, tap_table)

    return run
```

```python
import math

import jax
import jax.numpy as jnp
import ml_dtypes
import numpy as np
from jax import lax
from jax.experimental import pallas as pl
from jax.experimental.pallas import tpu as pltpu
from jax.sharding import PartitionSpec as P

NFFT = 2048
HALF = NFFT // 2
TAPS = 4
SPEC = 256
CHAN = 1024
GROUPS = 16
LOCAL_CHAN = CHAN // GROUPS
CHUNKS = 4
CHUNK_CHAN = LOCAL_CHAN // CHUNKS
FOLD_CHAN = CHUNK_CHAN // 2
TARGETS = 8
ROWS = 2 * TARGETS * FOLD_CHAN
HALF_SPEC = SPEC // 2
STEPS = 2 * CHUNKS
STEP_CHAN = 8
SLOTS = 3
PAIR_LAG = 2
PASS_LAG = 3
BACK_LAG = 4
F32 = jnp.float32
BF16 = jnp.bfloat16
MESH = pl.DeviceIdType.MESH


def dft_tables():
    core, chunk, parity, part, target, index = np.meshgrid(
        np.arange(2), np.arange(CHUNKS), np.arange(2), np.arange(2), np.arange(TARGETS), np.arange(FOLD_CHAN),
        indexing="ij",
    )
    channel = (target * 2 + core) * LOCAL_CHAN + chunk * CHUNK_CHAN + 2 * index + parity
    phase = (channel[..., None] * np.arange(HALF)) % NFFT
    angle = phase * (2.0 * np.pi / NFFT)
    cosine = np.where(phase % (NFFT // 2) == NFFT // 4, 0.0, np.cos(angle))
    sine = np.where(phase % (NFFT // 2) == 0, 0.0, np.sin(angle))
    values = np.where(part[..., None] == 0, cosine, -sine) / (64.0 * math.sqrt(NFFT) * 4096.0)
    high = values.astype(ml_dtypes.bfloat16)
    low = (values - high.astype(np.float64)).astype(ml_dtypes.bfloat16)
    shape = (2, CHUNKS, 2, ROWS, HALF)
    return np.concatenate([high.reshape(shape), low.reshape(shape)], axis=3)


def filter_half(half, source, first, taps_ref, frames, mixed, folded):
    count = 4 * (HALF_SPEC + TAPS - 1)

    @pl.loop(0, HALF // 128)
    def _(step):
        low = pl.multiple_of(step * 128, 128)
        columns = (low, pl.multiple_of(low + HALF, 128))
        weights = []
        for side in range(2):
            block = source[pl.ds(half * HALF_SPEC, HALF_SPEC + TAPS - 1), :, pl.ds(columns[side], 128)]
            frames[side, 0:count, :] = block.astype(F32).reshape(count, 128)
            weights.append([taps_ref[pl.ds(tap, 1), pl.ds(columns[side], 128)].astype(F32) for tap in range(TAPS)])
        for start in range(0, 4 * HALF_SPEC, 64):
            sides = []
            for side in range(2):
                even = frames[side, start : start + 72, :]
                odd = frames[side, start + 4 : start + 76, :]
                w = weights[side]
                sides.append(w[0] * even[:64] + w[1] * odd[:64] + w[2] * even[8:] + w[3] * odd[8:])
            mixed[0, start : start + 64, :] = sides[0] + sides[1]
            mixed[1, start : start + 64, :] = sides[0] - sides[1]
        for row in range(4):
            slot = first + row
            place = (slot % 2) * HALF_SPEC
            for parity in range(2):
                value = mixed[parity, pl.ds(row, HALF_SPEC, stride=4), :]
                top = value.astype(BF16)
                rest = (value - top.astype(F32)).astype(BF16)
                folded[parity, 0, half, slot // 2, place : place + HALF_SPEC, pl.ds(low, 128)] = top
                folded[parity, 1, half, slot // 2, place : place + HALF_SPEC, pl.ds(low, 128)] = rest


def transform_rows(half, quarter, core, table_ref, folded, turned, first_duo, last_duo):
    contract = (((1,), (1,)), ((), ()))

    @pl.loop(first_duo, last_duo)
    def _(duo):
        for parity in range(2):
            top = folded[parity, 0, half, duo]
            both = lax.dot_general(table_ref[quarter, parity], top, contract, preferred_element_type=F32)
            rest = lax.dot_general(
                table_ref[quarter, parity, :ROWS], folded[parity, 1, half, duo], contract, preferred_element_type=F32
            )
            value = both[:ROWS] + both[ROWS:] + rest
            for sub in range(2):
                row = lax.rem(2 * duo + sub + 4 * core, 8)
                for part in range(2):
                    turned[pl.ds(parity * 16 + part * 8 + row, ROWS // 2, stride=32), :] = value[
                        part * (ROWS // 2) : (part + 1) * (ROWS // 2), sub * 128 : sub * 128 + 128
                    ]


def round_rows(turned, write):
    block = CHUNK_CHAN * 16

    @pl.loop(0, TARGETS)
    def _(target):
        rows = turned[pl.ds(pl.multiple_of(target * block, block), block), :]
        write(target, rows.reshape(2 * CHUNK_CHAN, 8, 128).astype(BF16))


def stacked(real, imag):
    return jnp.concatenate([jnp.concatenate([real, imag], axis=1), jnp.concatenate([imag, -real], axis=1)], axis=0)


def exchange_kernel(
    own_ref, taps_ref, table_hbm, rows, near, far, crossed,
    own, other, table, frames, mixed, folded, turned, made, products,
    load_sem, table_sem, core_send, core_recv,
    local_sem, first_send, first_recv, pair_send, pair_recv, ring_send, ring_recv, pass_send, pass_recv,
    back_send, back_recv,
):
    freq, z, xl = lax.axis_index("freq"), lax.axis_index("row"), lax.axis_index("col")
    core = lax.rem(freq, 2)
    xh = lax.rem(freq // 2, 2)
    y = freq // 4
    up, down = lax.rem(z + 1, 4), lax.rem(z + 3, 4)
    pieces = (pl.ds(0, HALF_SPEC + TAPS - 1), pl.ds(HALF_SPEC + TAPS - 1, HALF_SPEC))

    def load(part):
        return pltpu.make_async_copy(own_ref.at[pieces[part]], own.at[pieces[part]], load_sem.at[part])

    def load_table(quarter):
        return pltpu.make_async_copy(table_hbm.at[core, quarter], table.at[quarter], table_sem.at[quarter])

    load(0).start()
    for quarter in range(CHUNKS):
        load_table(quarter).start()
    load(1).start()

    def device(to_y, to_xh, to_z, to_xl, to_core=core):
        return {"freq": (to_y * 2 + to_xh) * 2 + to_core, "row": to_z, "col": to_xl}

    sibling = device(y, xh, z, xl, 1 - core)
    partner = device(y, xh, z, 1 - xl)
    above, below = device(y, xh, up, xl), device(y, xh, down, xl)

    barrier = pltpu.get_barrier_semaphore()
    others = [sibling]
    others += [device(lax.rem(y + step, 4), xh, z, xl) for step in range(1, 4)]
    others += [device(lax.rem(y + step, 4), 1 - xh, z, 1 - xl) for step in range(4)]
    others += [partner, above, below, device(y, xh, up, 1 - xl), device(y, xh, down, 1 - xl)]
    for one in others:
        pl.semaphore_signal(barrier, inc=1, device_id=one, device_id_type=MESH)
    pl.semaphore_wait(barrier, len(others))

    def remote(source, target, send, recv, where):
        return pltpu.make_async_remote_copy(
            src_ref=source, dst_ref=target, send_sem=send, recv_sem=recv, device_id=where, device_id_type=MESH
        )

    def swap(part):
        return remote(
            own_ref.at[pieces[part]], other.at[pieces[part]], core_send.at[part], core_recv.at[part], sibling
        )

    for part in range(2):
        swap(part).start()

    def spot(t):
        return lax.rem(t, CHUNKS), pl.ds(pl.multiple_of((t // CHUNKS) * HALF_SPEC, HALF_SPEC), HALF_SPEC)

    def home(t, side, from_y, from_xh):
        k, lanes = spot(t)
        return rows.at[k, :, side, from_y, from_xh, :, lanes]

    def first(t, step, flip):
        to_y, to_xh, to_xl = lax.rem(y + step, 4), (1 - xh if flip else xh), (1 - xl if flip else xl)
        index = flip * 4 + step
        return remote(
            made.at[t, to_y * 2 + to_xh], home(t, xl, y, xh),
            first_send.at[t, index], first_recv.at[t, index], device(to_y, to_xh, z, to_xl),
        )

    def first_arrival(t, step, flip):
        from_y, from_xh, from_xl = lax.rem(y + 4 - step, 4), (1 - xh if flip else xh), (1 - xl if flip else xl)
        index = flip * 4 + step
        place = home(t, from_xl, from_y, from_xh)
        return remote(
            place, place, first_send.at[t, index], first_recv.at[t, index], device(from_y, from_xh, z, from_xl)
        )

    def local(t):
        return pltpu.make_async_copy(made.at[t, y * 2 + xh], home(t, xl, y, xh), local_sem.at[t])

    def pair(t, part, mine=True):
        k, lanes = spot(t)
        side = xl if (part == 0) == mine else 1 - xl
        place = rows.at[k, :, side, :, xh if part == 0 else 1 - xh, :, lanes]
        return remote(place, place, pair_send.at[t, part], pair_recv.at[t, part], partner)

    def ring(t, part, way):
        k, lanes = spot(t)
        column = xh if part == 0 else 1 - xh
        share = pl.ds(way * CHUNK_CHAN, CHUNK_CHAN)
        return remote(
            rows.at[k, share, xl, :, column, :, lanes], near.at[k, share, :, column, :, lanes],
            ring_send.at[t, part, way], ring_recv.at[t, part, way], above if way == 0 else below,
        )

    def onward(t, part, way):
        k, lanes = spot(t)
        column = xh if part == 0 else 1 - xh
        share = pl.ds(way * CHUNK_CHAN, CHUNK_CHAN)
        return remote(
            near.at[k, share, :, column, :, lanes], far.at[k, share, :, column, :, lanes],
            pass_send.at[t, part, way], pass_recv.at[t, part, way], above if way == 0 else below,
        )

    def back(k, way, side):
        share = pl.ds(way * FOLD_CHAN, FOLD_CHAN)
        return remote(
            products.at[k, side, share], crossed.at[xl, k, share],
            back_send.at[k, way, side], back_recv.at[k, way, xl],
            device(y, xh, down if way == 0 else up, side),
        )

    def back_arrival(k, way, side):
        share = pl.ds(way * FOLD_CHAN, FOLD_CHAN)
        place = crossed.at[side, k, share]
        return remote(
            place, place, back_send.at[k, way, side], back_recv.at[k, way, side],
            device(y, xh, up if way == 0 else down, side),
        )

    def multiply(k):
        for way in range(2):

            @pl.loop(way * FOLD_CHAN, (way + 1) * FOLD_CHAN)
            def _(c):
                left = [rows[k, 2 * c + part].reshape(128, SPEC) for part in range(2)]
                right = [near[k, 2 * c + part].reshape(64, SPEC) for part in range(2)]
                value = lax.dot_general(
                    jnp.concatenate(left, axis=1), stacked(right[0], right[1]), (((1,), (1,)), ((), ())),
                    preferred_element_type=F32,
                )
                value = (value * (1.0 / SPEC)).astype(BF16)
                products[k, 0, c] = value[:64]
                products[k, 1, c] = value[64:]

            for side in range(2):
                back(k, way, side).start()

    def fold_own(half):
        load(half).wait()
        filter_half(half, own, 0, taps_ref, frames, mixed, folded)

    def fold_other(half):
        swap(half).wait_recv()
        filter_half(half, other, 4, taps_ref, frames, mixed, folded)

    fold_own(0)
    load_table(0).wait()
    transform_rows(0, 0, core, table, folded, turned, 0, 2)
    fold_other(0)
    for quarter in range(1, CHUNKS):
        load_table(quarter).wait()

    @pl.loop(0, STEPS + BACK_LAG)
    def _(turn):
        @pl.when(turn == CHUNKS)
        def _():
            fold_own(1)
            fold_other(1)

        @pl.when(turn < STEPS)
        def _():
            def write(target, value):
                made[turn, target] = value

            first_duo = 2 - 2 * lax.min(turn, 1)
            transform_rows(turn // CHUNKS, lax.rem(turn, CHUNKS), core, table, folded, turned, first_duo, 4)
            round_rows(turned, write)
            local(turn).start()
            for step in range(1, 4):
                first(turn, step, 0).start()
            for step in range(4):
                first(turn, step, 1).start()

        @pl.when((turn >= 1) & (turn <= STEPS))
        def _():
            t = turn - 1
            local(t).wait()
            for step in range(1, 4):
                first_arrival(t, step, 0).wait_recv()
            for way in range(2):
                ring(t, 0, way).start()
            for step in range(4):
                first_arrival(t, step, 1).wait_recv()
            pair(t, 1).start()

        @pl.when((turn >= PAIR_LAG) & (turn < STEPS + PAIR_LAG))
        def _():
            t = turn - PAIR_LAG
            pair(t, 1, False).wait_recv()
            for way in range(2):
                ring(t, 1, way).start()

        @pl.when((turn >= PASS_LAG) & (turn < STEPS + PASS_LAG))
        def _():
            t = turn - PASS_LAG
            for part in range(2):
                for way in range(2):
                    ring(t, part, way).wait_recv()
                    onward(t, part, way).start()
            pair(t, 0, False).wait_recv()

        @pl.when((turn >= 1) & (turn <= STEPS))
        def _():
            pair(turn - 1, 0).start()

        @pl.when(turn >= CHUNKS + BACK_LAG)
        def _():
            multiply(turn - CHUNKS - BACK_LAG)

    for part in range(2):
        swap(part).wait_send()

    @pl.loop(0, CHUNKS)
    def _(k):
        for way in range(2):
            for side in range(2):
                back_arrival(k, way, side).wait_recv()
                back(k, way, side).wait_send()

    @pl.loop(0, STEPS)
    def _(t):
        for step in range(1, 4):
            first(t, step, 0).wait_send()
        for step in range(4):
            first(t, step, 1).wait_send()
        for part in range(2):
            pair(t, part).wait_send()
            for way in range(2):
                ring(t, part, way).wait_send()
                onward(t, part, way).wait_recv()
                onward(t, part, way).wait_send()


def exchange(voltages, taps, table):
    any_space = pl.BlockSpec(memory_space=pl.ANY)
    dma = pltpu.SemaphoreType.DMA
    return pl.pallas_call(
        exchange_kernel,
        in_specs=[any_space, pl.BlockSpec(memory_space=pltpu.VMEM), any_space],
        out_specs=[pl.BlockSpec(memory_space=pltpu.VMEM)] * 4,
        out_shape=[
            pltpu.VMEM((CHUNKS, 2 * CHUNK_CHAN, 2, 4, 2, 8, SPEC), BF16),
            pltpu.VMEM((CHUNKS, 2 * CHUNK_CHAN, 4, 2, 8, SPEC), BF16),
            pltpu.VMEM((CHUNKS, 2 * CHUNK_CHAN, 4, 2, 8, SPEC), BF16),
            pltpu.VMEM((2, CHUNKS, CHUNK_CHAN, 64, 128), BF16),
        ],
        scratch_shapes=[
            pltpu.VMEM(voltages.shape, BF16),
            pltpu.VMEM(voltages.shape, BF16),
            pltpu.VMEM(table.shape[1:], BF16),
            pltpu.VMEM((2, 4 * 132, 128), F32),
            pltpu.VMEM((2, 4 * HALF_SPEC, 128), F32),
            pltpu.VMEM((2, 2, 2, 4, 2 * HALF_SPEC, HALF), BF16),
            pltpu.VMEM((TARGETS * CHUNK_CHAN * 16, 128), F32),
            pltpu.VMEM((STEPS, TARGETS, 2 * CHUNK_CHAN, 8, HALF_SPEC), BF16),
            pltpu.VMEM((CHUNKS, 2, CHUNK_CHAN, 64, 128), BF16),
            dma((2,)),
            dma((CHUNKS,)),
            dma((2,)),
            dma((2,)),
            dma((STEPS,)),
            dma((STEPS, 8)),
            dma((STEPS, 8)),
            dma((STEPS, 2)),
            dma((STEPS, 2)),
            dma((STEPS, 2, 2)),
            dma((STEPS, 2, 2)),
            dma((STEPS, 2, 2)),
            dma((STEPS, 2, 2)),
            dma((CHUNKS, 2, 2)),
            dma((CHUNKS, 2, 2)),
        ],
        compiler_params=pltpu.CompilerParams(collective_id=0, has_side_effects=True, vmem_limit_bytes=40 << 20),
        name="exchange",
    )(voltages, taps, table)


def correlate_kernel(rows, near, far, crossed, out_hbm, out_ref, out_sem):
    z, xl = lax.axis_index("row"), lax.axis_index("col")
    groups = LOCAL_CHAN // STEP_CHAN

    def store(g):
        slot = lax.rem(g, SLOTS)
        return pltpu.make_async_copy(
            out_ref.at[slot], out_hbm.at[pl.ds(g * STEP_CHAN, STEP_CHAN)], out_sem.at[slot]
        )

    @pl.loop(0, groups)
    def _(g):
        @pl.when(g >= SLOTS)
        def _():
            store(g - SLOTS).wait()

        slot = lax.rem(g, SLOTS)
        k = g * STEP_CHAN // CHUNK_CHAN
        down_share = lax.rem(g // (FOLD_CHAN // STEP_CHAN), 2)
        near_plane = lax.rem(z + 3 + 2 * down_share, 4)
        far_plane = lax.rem(z + 2, 4)
        crossed_plane = lax.rem(z + 1 + 2 * down_share, 4)
        for c in range(STEP_CHAN):
            place = lax.rem(g * STEP_CHAN, CHUNK_CHAN) + c
            parts = []
            for part in range(2):
                pieces = [rows[k, 2 * place + part, xl], near[k, 2 * place + part], far[k, 2 * place + part]]
                parts.append(jnp.concatenate([piece.reshape(64, SPEC) for piece in pieces], axis=0))
            row_side = [rows[k, 2 * place + part].reshape(128, SPEC) for part in range(2)]
            both = lax.dot_general(
                jnp.concatenate(parts, axis=0), jnp.concatenate(row_side, axis=0), (((1,), (1,)), ((), ())),
                preferred_element_type=F32,
            )
            value = jnp.concatenate(
                [both[:192, :128] + both[192:, 128:], both[:192, 128:] - both[192:, :128]], axis=1
            ) * (1.0 / SPEC)
            for index, plane in enumerate((z, near_plane, far_plane)):
                out_ref[slot, c, 0, plane] = value[index * 64 : index * 64 + 64, :128]
                out_ref[slot, c, 1, plane] = value[index * 64 : index * 64 + 64, 128:]
            sides = [crossed[side, k, place].astype(F32) for side in range(2)]
            out_ref[slot, c, 0, crossed_plane] = jnp.concatenate([side[:, :64] for side in sides], axis=1)
            out_ref[slot, c, 1, crossed_plane] = jnp.concatenate([side[:, 64:] for side in sides], axis=1)
        store(g).start()

    @pl.loop(groups - SLOTS, groups)
    def _(g):
        store(g).wait()


def correlate(rows, near, far, crossed):
    return pl.pallas_call(
        correlate_kernel,
        in_specs=[pl.BlockSpec(memory_space=pltpu.VMEM)] * 4,
        out_specs=pl.BlockSpec(memory_space=pl.ANY),
        out_shape=jax.ShapeDtypeStruct((LOCAL_CHAN, 2, 4, 64, 128), F32),
        scratch_shapes=[
            pltpu.VMEM((SLOTS, STEP_CHAN, 2, 4, 64, 128), F32),
            pltpu.SemaphoreType.DMA((SLOTS,)),
        ],
        compiler_params=pltpu.CompilerParams(vmem_limit_bytes=20 << 20),
        name="correlate",
    )(rows, near, far, crossed)


def shards(table, voltages, tap_table):
    rows, near, far, crossed = exchange(jnp.transpose(voltages, (1, 0, 2)), tap_table, table)
    return correlate(rows, near, far, crossed)


def solution(mesh):
    table = dft_tables()

    def run(voltages, tap_table):
        return jax.shard_map(
            shards,
            mesh=mesh,
            in_specs=(P(), P(("row", "col", "freq"), None, None), P()),
            out_specs=P("freq", None, None, "col", "row"),
            check_vma=False,
        )(jnp.asarray(table), voltages, tap_table)

    return run
```

```python
import math

import jax
import jax.numpy as jnp
import ml_dtypes
import numpy as np
from jax import lax
from jax.experimental import pallas as pl
from jax.experimental.pallas import tpu as pltpu
from jax.sharding import PartitionSpec as P

NFFT = 2048
HALF = NFFT // 2
TAPS = 4
SPEC = 256
CHAN = 1024
GROUPS = 16
LOCAL_CHAN = CHAN // GROUPS
CHUNKS = 4
CHUNK_CHAN = LOCAL_CHAN // CHUNKS
FOLD_CHAN = CHUNK_CHAN // 2
TARGETS = 8
ROWS = 2 * TARGETS * FOLD_CHAN
HALF_SPEC = SPEC // 2
STEPS = 2 * CHUNKS
STEP_CHAN = 8
SLOTS = 3
PAIR_LAG = 2
PASS_LAG = 3
BACK_LAG = 4
F32 = jnp.float32
BF16 = jnp.bfloat16
MESH = pl.DeviceIdType.MESH


def dft_tables():
    core, chunk, parity, part, target, index = np.meshgrid(
        np.arange(2), np.arange(CHUNKS), np.arange(2), np.arange(2), np.arange(TARGETS), np.arange(FOLD_CHAN),
        indexing="ij",
    )
    channel = (target * 2 + core) * LOCAL_CHAN + chunk * CHUNK_CHAN + 2 * index + parity
    phase = (channel[..., None] * np.arange(HALF)) % NFFT
    angle = phase * (2.0 * np.pi / NFFT)
    cosine = np.where(phase % (NFFT // 2) == NFFT // 4, 0.0, np.cos(angle))
    sine = np.where(phase % (NFFT // 2) == 0, 0.0, np.sin(angle))
    values = np.where(part[..., None] == 0, cosine, -sine) / (64.0 * math.sqrt(NFFT) * 4096.0)
    high = values.astype(ml_dtypes.bfloat16)
    low = (values - high.astype(np.float64)).astype(ml_dtypes.bfloat16)
    shape = (2, CHUNKS, 2, ROWS, HALF)
    return np.concatenate([high.reshape(shape), low.reshape(shape)], axis=3)


def filter_half(half, source, first, taps_ref, frames, mixed, folded):
    count = 4 * (HALF_SPEC + TAPS - 1)

    @pl.loop(0, HALF // 128)
    def _(step):
        low = pl.multiple_of(step * 128, 128)
        columns = (low, pl.multiple_of(low + HALF, 128))
        weights = []
        for side in range(2):
            block = source[pl.ds(half * HALF_SPEC, HALF_SPEC + TAPS - 1), :, pl.ds(columns[side], 128)]
            frames[side, 0:count, :] = block.astype(F32).reshape(count, 128)
            weights.append([taps_ref[pl.ds(tap, 1), pl.ds(columns[side], 128)].astype(F32) for tap in range(TAPS)])
        for start in range(0, 4 * HALF_SPEC, 64):
            sides = []
            for side in range(2):
                even = frames[side, start : start + 72, :]
                odd = frames[side, start + 4 : start + 76, :]
                w = weights[side]
                sides.append(w[0] * even[:64] + w[1] * odd[:64] + w[2] * even[8:] + w[3] * odd[8:])
            mixed[0, start : start + 64, :] = sides[0] + sides[1]
            mixed[1, start : start + 64, :] = sides[0] - sides[1]
        for row in range(4):
            slot = first + row
            place = (slot % 2) * HALF_SPEC
            for parity in range(2):
                value = mixed[parity, pl.ds(row, HALF_SPEC, stride=4), :]
                top = value.astype(BF16)
                rest = (value - top.astype(F32)).astype(BF16)
                folded[parity, 0, half, slot // 2, place : place + HALF_SPEC, pl.ds(low, 128)] = top
                folded[parity, 1, half, slot // 2, place : place + HALF_SPEC, pl.ds(low, 128)] = rest


def transform_rows(half, quarter, core, table_ref, folded, turned, first_duo, last_duo):
    contract = (((1,), (1,)), ((), ()))

    @pl.loop(first_duo, last_duo)
    def _(duo):
        for parity in range(2):
            top = folded[parity, 0, half, duo]
            both = lax.dot_general(table_ref[quarter, parity], top, contract, preferred_element_type=F32)
            rest = lax.dot_general(
                table_ref[quarter, parity, :ROWS], folded[parity, 1, half, duo], contract, preferred_element_type=F32
            )
            value = both[:ROWS] + both[ROWS:] + rest
            for sub in range(2):
                row = lax.rem(2 * duo + sub + 4 * core, 8)
                for part in range(2):
                    turned[pl.ds(parity * 16 + part * 8 + row, ROWS // 2, stride=32), :] = value[
                        part * (ROWS // 2) : (part + 1) * (ROWS // 2), sub * 128 : sub * 128 + 128
                    ]


def round_rows(turned, write):
    block = CHUNK_CHAN * 16

    @pl.loop(0, TARGETS)
    def _(target):
        rows = turned[pl.ds(pl.multiple_of(target * block, block), block), :]
        write(target, rows.reshape(2 * CHUNK_CHAN, 8, 128).astype(BF16))


def exchange_kernel(
    own_ref, taps_ref, table_hbm, rows, near, far, crossed,
    own, other, table, frames, mixed, folded, turned, made, products,
    load_sem, table_sem, core_send, core_recv,
    local_sem, first_send, first_recv, pair_send, pair_recv, ring_send, ring_recv, pass_send, pass_recv,
    back_send, back_recv,
):
    freq, z, xl = lax.axis_index("freq"), lax.axis_index("row"), lax.axis_index("col")
    core = lax.rem(freq, 2)
    xh = lax.rem(freq // 2, 2)
    y = freq // 4
    up, down = lax.rem(z + 1, 4), lax.rem(z + 3, 4)
    pieces = (pl.ds(0, HALF_SPEC + TAPS - 1), pl.ds(HALF_SPEC + TAPS - 1, HALF_SPEC))

    def load(part):
        return pltpu.make_async_copy(own_ref.at[pieces[part]], own.at[pieces[part]], load_sem.at[part])

    def load_table(quarter):
        return pltpu.make_async_copy(table_hbm.at[core, quarter], table.at[quarter], table_sem.at[quarter])

    load(0).start()
    for quarter in range(CHUNKS):
        load_table(quarter).start()
    load(1).start()

    def device(to_y, to_xh, to_z, to_xl, to_core=core):
        return {"freq": (to_y * 2 + to_xh) * 2 + to_core, "row": to_z, "col": to_xl}

    sibling = device(y, xh, z, xl, 1 - core)
    partner = device(y, xh, z, 1 - xl)
    above, below = device(y, xh, up, xl), device(y, xh, down, xl)

    barrier = pltpu.get_barrier_semaphore()
    others = [sibling]
    others += [device(lax.rem(y + step, 4), xh, z, xl) for step in range(1, 4)]
    others += [device(lax.rem(y + step, 4), 1 - xh, z, 1 - xl) for step in range(4)]
    others += [partner, above, below, device(y, xh, up, 1 - xl), device(y, xh, down, 1 - xl)]
    for one in others:
        pl.semaphore_signal(barrier, inc=1, device_id=one, device_id_type=MESH)
    pl.semaphore_wait(barrier, len(others))

    def remote(source, target, send, recv, where):
        return pltpu.make_async_remote_copy(
            src_ref=source, dst_ref=target, send_sem=send, recv_sem=recv, device_id=where, device_id_type=MESH
        )

    def swap(part):
        return remote(
            own_ref.at[pieces[part]], other.at[pieces[part]], core_send.at[part], core_recv.at[part], sibling
        )

    for part in range(2):
        swap(part).start()

    def spot(t):
        return lax.rem(t, CHUNKS), pl.ds(pl.multiple_of((t // CHUNKS) * HALF_SPEC, HALF_SPEC), HALF_SPEC)

    def home(t, side, from_y, from_xh):
        k, lanes = spot(t)
        return rows.at[k, :, side, from_y, from_xh, :, lanes]

    def first(t, step, flip):
        to_y, to_xh, to_xl = lax.rem(y + step, 4), (1 - xh if flip else xh), (1 - xl if flip else xl)
        index = flip * 4 + step
        return remote(
            made.at[t, to_y * 2 + to_xh], home(t, xl, y, xh),
            first_send.at[t, index], first_recv.at[t, index], device(to_y, to_xh, z, to_xl),
        )

    def first_arrival(t, step, flip):
        from_y, from_xh, from_xl = lax.rem(y + 4 - step, 4), (1 - xh if flip else xh), (1 - xl if flip else xl)
        index = flip * 4 + step
        place = home(t, from_xl, from_y, from_xh)
        return remote(
            place, place, first_send.at[t, index], first_recv.at[t, index], device(from_y, from_xh, z, from_xl)
        )

    def local(t):
        return pltpu.make_async_copy(made.at[t, y * 2 + xh], home(t, xl, y, xh), local_sem.at[t])

    def pair(t, part, mine=True):
        k, lanes = spot(t)
        side = xl if (part == 0) == mine else 1 - xl
        place = rows.at[k, :, side, :, xh if part == 0 else 1 - xh, :, lanes]
        return remote(place, place, pair_send.at[t, part], pair_recv.at[t, part], partner)

    def ring(t, part, way):
        k, lanes = spot(t)
        column = xh if part == 0 else 1 - xh
        share = pl.ds(way * CHUNK_CHAN, CHUNK_CHAN)
        return remote(
            rows.at[k, share, xl, :, column, :, lanes], near.at[k, share, :, column, :, lanes],
            ring_send.at[t, part, way], ring_recv.at[t, part, way], above if way == 0 else below,
        )

    def onward(t, part, way):
        k, lanes = spot(t)
        column = xh if part == 0 else 1 - xh
        share = pl.ds(way * CHUNK_CHAN, CHUNK_CHAN)
        return remote(
            near.at[k, share, :, column, :, lanes], far.at[k, share, :, column, :, lanes],
            pass_send.at[t, part, way], pass_recv.at[t, part, way], above if way == 0 else below,
        )

    def back(k, way, side):
        share = pl.ds(way * FOLD_CHAN, FOLD_CHAN)
        return remote(
            products.at[k, side, share], crossed.at[xl, k, share],
            back_send.at[k, way, side], back_recv.at[k, way, xl],
            device(y, xh, down if way == 0 else up, side),
        )

    def back_arrival(k, way, side):
        share = pl.ds(way * FOLD_CHAN, FOLD_CHAN)
        place = crossed.at[side, k, share]
        return remote(
            place, place, back_send.at[k, way, side], back_recv.at[k, way, side],
            device(y, xh, up if way == 0 else down, side),
        )

    def multiply(k):
        for way in range(2):

            @pl.loop(way * FOLD_CHAN, (way + 1) * FOLD_CHAN)
            def _(c):
                left = [rows[k, 2 * c + part].reshape(128, SPEC) for part in range(2)]
                right = [near[k, 2 * c + part].reshape(64, SPEC) for part in range(2)]
                both = lax.dot_general(
                    jnp.concatenate(left, axis=0), jnp.concatenate(right, axis=0), (((1,), (1,)), ((), ())),
                    preferred_element_type=F32,
                )
                real = both[:128, :64] + both[128:, 64:]
                imag = both[:128, 64:] - both[128:, :64]
                value = (jnp.concatenate([real, imag], axis=1) * (1.0 / SPEC)).astype(BF16)
                products[k, 0, c] = value[:64]
                products[k, 1, c] = value[64:]

            for side in range(2):
                back(k, way, side).start()

    def fold_own(half):
        load(half).wait()
        filter_half(half, own, 0, taps_ref, frames, mixed, folded)

    def fold_other(half):
        swap(half).wait_recv()
        filter_half(half, other, 4, taps_ref, frames, mixed, folded)

    fold_own(0)
    load_table(0).wait()
    transform_rows(0, 0, core, table, folded, turned, 0, 2)
    fold_other(0)
    for quarter in range(1, CHUNKS):
        load_table(quarter).wait()

    @pl.loop(0, STEPS + BACK_LAG)
    def _(turn):
        @pl.when(turn == CHUNKS)
        def _():
            fold_own(1)
            fold_other(1)

        @pl.when(turn < STEPS)
        def _():
            def write(target, value):
                made[turn, target] = value

            first_duo = 2 - 2 * lax.min(turn, 1)
            transform_rows(turn // CHUNKS, lax.rem(turn, CHUNKS), core, table, folded, turned, first_duo, 4)
            round_rows(turned, write)
            local(turn).start()
            for step in range(1, 4):
                first(turn, step, 0).start()
            for step in range(4):
                first(turn, step, 1).start()

        @pl.when((turn >= 1) & (turn <= STEPS))
        def _():
            t = turn - 1
            local(t).wait()
            for step in range(1, 4):
                first_arrival(t, step, 0).wait_recv()
            for way in range(2):
                ring(t, 0, way).start()
            for step in range(4):
                first_arrival(t, step, 1).wait_recv()
            pair(t, 1).start()

        @pl.when((turn >= PAIR_LAG) & (turn < STEPS + PAIR_LAG))
        def _():
            t = turn - PAIR_LAG
            pair(t, 1, False).wait_recv()
            for way in range(2):
                ring(t, 1, way).start()

        @pl.when((turn >= PASS_LAG) & (turn < STEPS + PASS_LAG))
        def _():
            t = turn - PASS_LAG
            for part in range(2):
                for way in range(2):
                    ring(t, part, way).wait_recv()
                    onward(t, part, way).start()
            pair(t, 0, False).wait_recv()

        @pl.when((turn >= 1) & (turn <= STEPS))
        def _():
            pair(turn - 1, 0).start()

        @pl.when(turn >= CHUNKS + BACK_LAG)
        def _():
            multiply(turn - CHUNKS - BACK_LAG)

    for part in range(2):
        swap(part).wait_send()

    @pl.loop(0, CHUNKS)
    def _(k):
        for way in range(2):
            for side in range(2):
                back_arrival(k, way, side).wait_recv()
                back(k, way, side).wait_send()

    @pl.loop(0, STEPS)
    def _(t):
        for step in range(1, 4):
            first(t, step, 0).wait_send()
        for step in range(4):
            first(t, step, 1).wait_send()
        for part in range(2):
            pair(t, part).wait_send()
            for way in range(2):
                ring(t, part, way).wait_send()
                onward(t, part, way).wait_recv()
                onward(t, part, way).wait_send()


def exchange(voltages, taps, table):
    any_space = pl.BlockSpec(memory_space=pl.ANY)
    dma = pltpu.SemaphoreType.DMA
    return pl.pallas_call(
        exchange_kernel,
        in_specs=[any_space, pl.BlockSpec(memory_space=pltpu.VMEM), any_space],
        out_specs=[pl.BlockSpec(memory_space=pltpu.VMEM)] * 4,
        out_shape=[
            pltpu.VMEM((CHUNKS, 2 * CHUNK_CHAN, 2, 4, 2, 8, SPEC), BF16),
            pltpu.VMEM((CHUNKS, 2 * CHUNK_CHAN, 4, 2, 8, SPEC), BF16),
            pltpu.VMEM((CHUNKS, 2 * CHUNK_CHAN, 4, 2, 8, SPEC), BF16),
            pltpu.VMEM((2, CHUNKS, CHUNK_CHAN, 64, 128), BF16),
        ],
        scratch_shapes=[
            pltpu.VMEM(voltages.shape, BF16),
            pltpu.VMEM(voltages.shape, BF16),
            pltpu.VMEM(table.shape[1:], BF16),
            pltpu.VMEM((2, 4 * 132, 128), F32),
            pltpu.VMEM((2, 4 * HALF_SPEC, 128), F32),
            pltpu.VMEM((2, 2, 2, 4, 2 * HALF_SPEC, HALF), BF16),
            pltpu.VMEM((TARGETS * CHUNK_CHAN * 16, 128), F32),
            pltpu.VMEM((STEPS, TARGETS, 2 * CHUNK_CHAN, 8, HALF_SPEC), BF16),
            pltpu.VMEM((CHUNKS, 2, CHUNK_CHAN, 64, 128), BF16),
            dma((2,)),
            dma((CHUNKS,)),
            dma((2,)),
            dma((2,)),
            dma((STEPS,)),
            dma((STEPS, 8)),
            dma((STEPS, 8)),
            dma((STEPS, 2)),
            dma((STEPS, 2)),
            dma((STEPS, 2, 2)),
            dma((STEPS, 2, 2)),
            dma((STEPS, 2, 2)),
            dma((STEPS, 2, 2)),
            dma((CHUNKS, 2, 2)),
            dma((CHUNKS, 2, 2)),
        ],
        compiler_params=pltpu.CompilerParams(collective_id=0, has_side_effects=True, vmem_limit_bytes=40 << 20),
        name="exchange",
    )(voltages, taps, table)


def correlate_kernel(rows, near, far, crossed, out_hbm, out_ref, out_sem):
    z, xl = lax.axis_index("row"), lax.axis_index("col")
    groups = LOCAL_CHAN // STEP_CHAN

    def store(g):
        slot = lax.rem(g, SLOTS)
        return pltpu.make_async_copy(
            out_ref.at[slot], out_hbm.at[pl.ds(g * STEP_CHAN, STEP_CHAN)], out_sem.at[slot]
        )

    @pl.loop(0, groups)
    def _(g):
        @pl.when(g >= SLOTS)
        def _():
            store(g - SLOTS).wait()

        slot = lax.rem(g, SLOTS)
        k = g * STEP_CHAN // CHUNK_CHAN
        down_share = lax.rem(g // (FOLD_CHAN // STEP_CHAN), 2)
        near_plane = lax.rem(z + 3 + 2 * down_share, 4)
        far_plane = lax.rem(z + 2, 4)
        crossed_plane = lax.rem(z + 1 + 2 * down_share, 4)
        for c in range(STEP_CHAN):
            place = lax.rem(g * STEP_CHAN, CHUNK_CHAN) + c
            parts = []
            for part in range(2):
                pieces = [rows[k, 2 * place + part, xl], near[k, 2 * place + part], far[k, 2 * place + part]]
                parts.append(jnp.concatenate([piece.reshape(64, SPEC) for piece in pieces], axis=0))
            row_side = [rows[k, 2 * place + part].reshape(128, SPEC) for part in range(2)]
            both = lax.dot_general(
                jnp.concatenate(parts, axis=0), jnp.concatenate(row_side, axis=0), (((1,), (1,)), ((), ())),
                preferred_element_type=F32,
            )
            value = jnp.concatenate(
                [both[:192, :128] + both[192:, 128:], both[:192, 128:] - both[192:, :128]], axis=1
            ) * (1.0 / SPEC)
            for index, plane in enumerate((z, near_plane, far_plane)):
                out_ref[slot, c, 0, plane] = value[index * 64 : index * 64 + 64, :128]
                out_ref[slot, c, 1, plane] = value[index * 64 : index * 64 + 64, 128:]
            sides = [crossed[side, k, place].astype(F32) for side in range(2)]
            out_ref[slot, c, 0, crossed_plane] = jnp.concatenate([side[:, :64] for side in sides], axis=1)
            out_ref[slot, c, 1, crossed_plane] = jnp.concatenate([side[:, 64:] for side in sides], axis=1)
        store(g).start()

    @pl.loop(groups - SLOTS, groups)
    def _(g):
        store(g).wait()


def correlate(rows, near, far, crossed):
    return pl.pallas_call(
        correlate_kernel,
        in_specs=[pl.BlockSpec(memory_space=pltpu.VMEM)] * 4,
        out_specs=pl.BlockSpec(memory_space=pl.ANY),
        out_shape=jax.ShapeDtypeStruct((LOCAL_CHAN, 2, 4, 64, 128), F32),
        scratch_shapes=[
            pltpu.VMEM((SLOTS, STEP_CHAN, 2, 4, 64, 128), F32),
            pltpu.SemaphoreType.DMA((SLOTS,)),
        ],
        compiler_params=pltpu.CompilerParams(vmem_limit_bytes=20 << 20),
        name="correlate",
    )(rows, near, far, crossed)


def shards(table, voltages, tap_table):
    rows, near, far, crossed = exchange(jnp.transpose(voltages, (1, 0, 2)), tap_table, table)
    return correlate(rows, near, far, crossed)


def solution(mesh):
    table = dft_tables()

    def run(voltages, tap_table):
        return jax.shard_map(
            shards,
            mesh=mesh,
            in_specs=(P(), P(("row", "col", "freq"), None, None), P()),
            out_specs=P("freq", None, None, "col", "row"),
            check_vma=False,
        )(jnp.asarray(table), voltages, tap_table)

    return run
```
